32 devices in a mesh: row: 8 (over z, y), col: 4 (over x, core).
Axes of the slice: x: 2, y: 2, z: 4, core: 2. Of those that a mesh axis runs over, the one named last changes fastest.
Arguments:
- panel_col: float32 [16384, 256], P('row', 'col'), may hold values from -6 to 6
- look_cols: float32 [16384, 2048], P('row', 'col'), may hold values from -6 to 6
- sketch_map: float32 [256, 16384], P(None, 'row'), may hold values from -0.046875 to 0.046875
- upper_inv: float32 [256, 256], replicated, may hold values from -0.09375 to 0.09375
- lower_inv: float32 [256, 256], replicated, may hold values from -0.375 to 0.375
- pivots: int32 [256], replicated, may hold values from 256 to 16383, as said below
Outputs:
- l_panel: float32 [16384, 256], P('row', 'col')
- updated: float32 [16384, 2048], P('row', 'col')
- sketch: float32 [256, 256], P(None, 'col')
The draws below stay inside these ranges and needn't reach their ends.
Inputs may be any that keep to these rules, and one draw needn't show every extreme that they name: `pivots`: distinct rows, none of them among the first 256.
All inputs are finite; a program needn't handle non-finite values.
Results may differ from the reference program's by a relative error of at most 0.000073.
Values sent between devices are 32-bit elements; how exact they have to be, the bound alone decides.
No kernel may reach another device: no remote copies, remote signals or barrier semaphores. Data moves between devices by JAX's collectives and lax.ppermute only.
A program may use at most 64 MiB of HBM per device.

```python
import jax
import jax.numpy as jnp
from jax import lax

NB = 256
W = 2048
KS = 256
ROWS_DEV = 2048
M = 16384


def draw_pivots(key, part):
    dev_count = M // ROWS_DEV
    base = jax.random.fold_in(key, 7)
    key_order, key_hot, key_one = jax.random.split(base, 3)
    order = jax.random.permutation(key_order, M).astype(jnp.int32)
    row_ids = jnp.arange(M, dtype=jnp.int32)
    dev_of = row_ids // ROWS_DEV
    hot_dev = jax.random.randint(key_hot, (dev_count,), 0, 4) == 0
    hot_dev = hot_dev | (jnp.arange(dev_count) == jax.random.randint(key_one, (), 0, dev_count))
    score = order + M * hot_dev[dev_of].astype(jnp.int32)
    score = jnp.where(row_ids < NB, -1 - row_ids, score)
    return lax.top_k(score, NB)[1].astype(jnp.int32)


def shard_levels(stream_key, shape, cuts, least, largest):
    level, own = 1.0, jax.random.fold_in(stream_key, 6)
    for dim, blocks in cuts:
        draws = jnp.exp(jax.random.uniform(jax.random.fold_in(own, dim), (blocks,), jnp.float32, least / len(cuts), largest / len(cuts)))
        level = level * jnp.repeat(draws, shape[dim] // blocks).reshape([-1 if axis == dim else 1 for axis in range(len(shape))])
    return level


def centred(own_key, shape, spread, most, cuts=(), kind=jnp.bfloat16):
    drawn = spread * jax.random.normal(own_key, shape, jnp.float32)
    if cuts:
        drawn = drawn * shard_levels(own_key, shape, cuts, -0.22, 0.18)
    return jnp.clip(drawn, -most, most).astype(kind)


def setup_inputs(seed: int = 0) -> dict:
    key_of = jax.random.split(jax.random.key(seed), 7)
    panel_col = centred(key_of[0], (M, NB), 1.0, 6.0, ((0, 8), (1, 4)), jnp.float32)
    look_cols = centred(key_of[1], (M, W), 1.0, 6.0, ((0, 8), (1, 4)), jnp.float32)
    sketch_map = centred(key_of[2], (KS, M), M ** -0.5, 0.046875, ((1, 8),), jnp.float32)
    upper_inv = centred(key_of[3], (NB, NB), (16 * NB) ** -0.5, 0.09375, (), jnp.float32)
    lower_inv = centred(key_of[4], (NB, NB), NB ** -0.5, 0.375, (), jnp.float32)
    pivots = draw_pivots(jax.random.fold_in(key_of[6], 71), 0)
    return {"panel_col": panel_col, "look_cols": look_cols, "sketch_map": sketch_map, "upper_inv": upper_inv, "lower_inv": lower_inv, "pivots": pivots}


high_prec = lax.Precision.HIGHEST


def swap_rows(matrix, pivots):
    initial = matrix[:NB]
    picked = matrix[pivots]
    return matrix.at[:NB].set(picked).at[pivots].set(initial)


def reference(panel_col, look_cols, sketch_map, upper_inv, lower_inv, pivots):
    sketch = jnp.dot(sketch_map, panel_col, precision=high_prec, preferred_element_type=jnp.float32)
    swapped_panel = swap_rows(panel_col, pivots)
    swapped_look = swap_rows(look_cols, pivots)
    upper_tri = jnp.triu(upper_inv)
    lower_tri = jnp.tril(lower_inv, -1) + jnp.eye(NB, dtype=jnp.float32)
    factor = jnp.dot(swapped_panel, upper_tri, precision=high_prec, preferred_element_type=jnp.float32)
    is_top = (jnp.arange(M) < NB)[:, None]
    l_panel = jnp.where(is_top, swapped_panel, factor)
    u_rows = jnp.dot(lower_tri, swapped_look[:NB], precision=high_prec, preferred_element_type=jnp.float32)
    updated = swapped_look - jnp.dot(factor, u_rows, precision=high_prec, preferred_element_type=jnp.float32)
    updated = updated.at[:NB].set(u_rows)
    return l_panel, updated, sketch
```

```python
import functools

import jax
import jax.numpy as jnp
from jax import lax
from jax.experimental import pallas as pl
from jax.experimental.pallas import tpu as pltpu
from jax.sharding import PartitionSpec as P

F32, BF16, I32 = jnp.float32, jnp.bfloat16, jnp.int32
GROUP = 4
VMEM = pl.BlockSpec(memory_space=pltpu.VMEM)
SMEM = pl.BlockSpec(memory_space=pltpu.SMEM)
HBM = pl.BlockSpec(memory_space=pl.ANY)


def split2(x):
    hi = x.astype(BF16)
    return hi, (x - hi.astype(F32)).astype(BF16)


def split3(x):
    hi = x.astype(BF16)
    rest = x - hi.astype(F32)
    mid = rest.astype(BF16)
    return hi, mid, (rest - mid.astype(F32)).astype(BF16)


def mm(a, b, dims=((1,), (0,))):
    return lax.dot_general(a, b, (dims, ((), ())), preferred_element_type=F32)


def mm3(a, b, dims=((1,), (0,))):
    return mm(a[0], b[0], dims) + (mm(a[0], b[1], dims) + mm(a[1], b[0], dims))


def pick_kernel(tab, pos, look, panel, sketch_map, target, *rest):
    outs, (owned_list, extra, sem) = rest[:GROUP], rest[GROUP:]
    slots = target.shape[0]
    chunk = slots // GROUP
    extra_rows = extra.shape[0] // GROUP
    q = pos[1]
    nt = ((1,), (1,))
    for s in range(GROUP):
        base = (q ^ s) * chunk

        @pl.loop(0, chunk, unroll=8)
        def _(i, s=s, base=base):
            pltpu.make_async_copy(
                look.at[pl.ds(tab[base + i], 1), :], outs[s].at[pl.ds(i, 1), :], sem.at[s]
            ).start()

    def note(p, count):
        owned_list[count] = p
        return count + tab[slots + p]

    count = lax.fori_loop(0, slots, note, jnp.int32(0), unroll=8)
    owned_list[slots] = count

    width = panel.shape[1]
    step = min(512, width)
    sketch_sum = jnp.zeros((panel.shape[0], sketch_map.shape[0]), F32)
    pick_sum = jnp.zeros((panel.shape[0], slots), F32)
    for k in range(0, width, step):
        hi, mid, lo = split3(panel[:, k : k + step])
        sketch_sum += mm3((hi, mid), split2(sketch_map[:, k : k + step]), nt)
        column = lax.broadcasted_iota(I32, (slots, step), 1) + k
        hot = jnp.where(column == target[...], 1.0, 0.0).astype(BF16)
        pick_sum += (mm(hi, hot, nt) + mm(mid, hot, nt)) + mm(lo, hot, nt)
    split = sketch_map.shape[0]
    extra[:, :split] = sketch_sum
    extra[:, split:] = pick_sum
    for s in range(GROUP):
        rows = pl.ds(pl.multiple_of((q ^ s) * extra_rows, 8), extra_rows)
        outs[s][chunk : chunk + extra_rows, :] = extra[rows, :]
    for s in range(GROUP):
        pltpu.make_async_copy(
            look.at[pl.ds(0, chunk), :], outs[s].at[pl.ds(0, chunk), :], sem.at[s]
        ).wait()


def swap_kernel(panel, head, target, out):
    slots = target.shape[0]
    hi, mid, lo = split3(head[...])
    ones = jnp.ones((16, slots), BF16)
    width = panel.shape[1]
    step = min(512, width)
    for k in range(0, width, step):
        column = lax.broadcasted_iota(I32, (slots, step), 1) + k
        hot = jnp.where(column == target[...], 1.0, 0.0).astype(BF16)
        moved = (mm(hi, hot) + mm(mid, hot)) + mm(lo, hot)
        hit = mm(ones, hot)[:1, :] > 0.5
        out[:, k : k + step] = jnp.where(hit, moved, panel[:, k : k + step])


def factor_kernel(pos, *rest):
    blocks, (upper, upper_own, fac_hi, fac_lo, own_out, whole) = rest[:-6], rest[-6:]
    cw = blocks[0].shape[0]
    for k, block in enumerate(blocks):
        rows = pl.ds(pl.multiple_of((pos[2] ^ k) * cw, 8), cw)
        whole[rows, :] = block[...]
    nb = upper.shape[0]
    keep = lax.broadcasted_iota(I32, (nb, nb), 0) <= lax.broadcasted_iota(I32, (nb, nb), 1)
    tri = split2(jnp.where(keep, upper[...], 0.0))
    data = whole[...]
    fac = mm3(split2(data.T), tri)
    hi, lo = split2(fac)
    fac_hi[...] = hi
    fac_lo[...] = lo
    own_out[...] = mm3(split2(upper_own[...]), split2(data))


def final_kernel(pos, owned_list, tab, look, fac_hi, fac_lo, lower, target, *rest):
    picks, spread = rest[:GROUP], rest[GROUP : 2 * GROUP]
    _, updated, panel_out, sketch_out, buf, piv, got, extra, in_sem, out_sem, top_sem = rest[2 * GROUP :]
    row, q = pos[0], pos[1]
    slots = target.shape[0]
    chunk = slots // GROUP
    rows_dev = buf.shape[0]
    extra_rows = extra.shape[0] // GROUP
    blocks = rows_dev // slots

    def load(b):
        part = pl.ds(b * slots, slots)
        return pltpu.make_async_copy(look.at[part, :], buf.at[part, :], in_sem.at[b])

    def store(b):
        part = pl.ds(b * slots, slots)
        return pltpu.make_async_copy(buf.at[part, :], updated.at[part, :], out_sem.at[b])

    for b in range(blocks):
        load(b).start()
    for s in range(GROUP):
        part = pl.ds(pl.multiple_of((q ^ s) * chunk, 8), chunk)
        mine = target[part, :] >= 0
        there = spread[s][:chunk, :]
        piv[part, :] = jnp.where(mine, picks[s][:chunk, :], there)
        got[part, :] = there
        erows = pl.ds(pl.multiple_of((q ^ s) * extra_rows, 8), extra_rows)
        extra[erows, :] = spread[s][chunk : chunk + extra_rows, :]
    split = sketch_out.shape[1]
    sketch_out[...] = extra[:, :split]

    below = lax.broadcasted_iota(I32, (slots, slots), 0) > lax.broadcasted_iota(I32, (slots, slots), 1)
    low = split2(jnp.where(below, lower[...], 0.0))
    first = piv[...]
    u_rows = first + mm3(low, split2(first))
    u_hi, u_lo = split2(u_rows)

    for b in range(blocks):
        load(b).wait()

    count = owned_list[slots]

    def place(source):
        @pl.loop(0, count)
        def _(k):
            p = owned_list[k]
            buf[pl.ds(tab[p], 1), :] = source[pl.ds(p, 1), :]

    @pl.when(row == 0)
    def _():
        place(buf)

    @pl.when(row != 0)
    def _():
        place(got)

    for b in range(blocks):
        part = pl.ds(b * slots, slots)
        drop = mm3((fac_hi[part, :], fac_lo[part, :]), (u_hi, u_lo))
        new = buf[part, :] - drop
        if b == 0:
            new = jnp.where(row == 0, u_rows, new)
        buf[part, :] = new
        store(b).start()

    top = pltpu.make_async_copy(
        extra.at[:, pl.ds(split, slots)], panel_out.at[:, pl.ds(0, slots)], top_sem
    )

    @pl.when(row == 0)
    def _():
        top.start()
        top.wait()

    for b in range(blocks):
        store(b).wait()


def on_device(n_row, n_col, panel_col, look_cols, sketch_map, upper_inv, lower_inv, pivots):
    rows_dev, cw = panel_col.shape
    lw = look_cols.shape[1]
    nb, ks = upper_inv.shape[0], sketch_map.shape[0]
    chunk, extra_rows = nb // GROUP, cw // GROUP
    assert ks + nb == lw and n_row % GROUP == 0
    assert n_row & (n_row - 1) == 0 and n_col & (n_col - 1) == 0
    row, col = lax.axis_index("row"), lax.axis_index("col")
    q = row % GROUP
    pos = jnp.stack([row, q, col]).astype(I32)
    panel_t = panel_col.T
    owner = pivots // rows_dev
    owned = owner == row
    local = pivots - row * rows_dev
    source = jnp.where(owned, local, jnp.arange(nb, dtype=I32))
    tab = jnp.concatenate([source, owned.astype(I32)])
    target = jnp.where(owned, local, -1)[:, None]

    def across(v, s):
        return lax.ppermute(v, "row", [(i, i ^ s) for i in range(n_row)])

    head = panel_t[:, :nb]
    bit = n_row // 2
    while bit:
        sent = lax.ppermute(head, "row", [(i, i + bit) for i in range(0, n_row, 2 * bit)])
        head = jnp.where(row % (2 * bit) == bit, sent, head)
        bit //= 2

    message = jax.ShapeDtypeStruct((chunk + extra_rows, lw), F32)
    *picks, owned_list = pl.pallas_call(
        pick_kernel,
        out_shape=[message] * GROUP + [jax.ShapeDtypeStruct((nb + 8,), I32)],
        in_specs=[SMEM, SMEM, HBM, VMEM, VMEM, VMEM],
        out_specs=[VMEM] * GROUP + [SMEM],
        scratch_shapes=[pltpu.VMEM((cw, lw), F32), pltpu.SemaphoreType.DMA((GROUP,))],
        cost_estimate=pl.CostEstimate(flops=10**9, bytes_accessed=4 * 10**6, transcendentals=0),
        name="pick",
    )(tab, pos, look_cols, panel_t, sketch_map, target)

    slot_owner = lax.dynamic_slice_in_dim(owner, q * chunk, chunk)
    slot_owner = jnp.concatenate([slot_owner, jnp.full((extra_rows,), -1, I32)])[:, None]
    summed = slot_owner < 0
    got = [picks[0]] + [across(picks[s], s) for s in range(1, GROUP)]
    have = sum(jnp.where(summed | (slot_owner == (row ^ s)), got[s], 0.0) for s in range(GROUP))
    top = got[0]
    for s in range(1, GROUP):
        top = jnp.where(row == s, got[s], top)
    bit = GROUP
    while bit < n_row:
        inside = summed | (slot_owner // bit == row // bit)
        got = across(jnp.where(inside, have, top), bit)
        other = (row // bit) ^ 1
        theirs = slot_owner // bit == other
        have = jnp.where(theirs, 0.0, have) + jnp.where(summed | theirs, got, 0.0)
        top = jnp.where(other == 0, got, top)
        bit *= 2
    spread = [jnp.where(slot_owner == (row ^ s), top, have) for s in range(GROUP)]
    spread = spread[:1] + [across(spread[s], s) for s in range(1, GROUP)]

    swapped = pl.pallas_call(
        swap_kernel,
        out_shape=jax.ShapeDtypeStruct((cw, rows_dev), F32),
        in_specs=[VMEM, VMEM, VMEM],
        out_specs=VMEM,
        cost_estimate=pl.CostEstimate(flops=2 * 10**8, bytes_accessed=10**6, transcendentals=0),
        name="swap",
    )(panel_t, head, target)

    blocks = {0: swapped}
    bit = n_col // 2
    while bit:
        for k in list(blocks):
            blocks[k ^ bit] = lax.ppermute(blocks[k], "col", [(i, i ^ bit) for i in range(n_col)])
        bit //= 2
    blocks = [blocks[k] for k in range(n_col)]
    upper_own = lax.dynamic_slice_in_dim(jnp.triu(upper_inv), col * cw, cw, 1).T

    step = min(nb, rows_dev)
    lane_block = pl.BlockSpec((cw, step), lambda b: (0, b))
    whole_block = lambda shape: pl.BlockSpec(shape, lambda b: (0, 0))
    row_block = pl.BlockSpec((step, nb), lambda b: (b, 0))
    fac_hi, fac_lo, panel_out = pl.pallas_call(
        factor_kernel,
        grid=(rows_dev // step,),
        out_shape=[
            jax.ShapeDtypeStruct((rows_dev, nb), BF16),
            jax.ShapeDtypeStruct((rows_dev, nb), BF16),
            jax.ShapeDtypeStruct((cw, rows_dev), F32),
        ],
        in_specs=[SMEM] + [lane_block] * n_col + [whole_block((nb, nb)), whole_block((cw, nb))],
        out_specs=[row_block, row_block, lane_block],
        scratch_shapes=[pltpu.VMEM((nb, step), F32)],
        cost_estimate=pl.CostEstimate(flops=10**9, bytes_accessed=6 * 10**6, transcendentals=0),
        name="factor",
    )(pos, *blocks, upper_inv, upper_own)

    n_in = 8 + 2 * GROUP
    updated, panel_out, sketch_t = pl.pallas_call(
        final_kernel,
        out_shape=[
            jax.ShapeDtypeStruct((rows_dev, lw), F32),
            jax.ShapeDtypeStruct((cw, rows_dev), F32),
            jax.ShapeDtypeStruct((cw, ks), F32),
        ],
        in_specs=[SMEM, SMEM, SMEM, HBM] + [VMEM] * (4 + 2 * GROUP) + [HBM],
        out_specs=[HBM, HBM, VMEM],
        input_output_aliases={n_in: 1},
        scratch_shapes=[
            pltpu.VMEM((rows_dev, lw), F32),
            pltpu.VMEM((nb, lw), F32),
            pltpu.VMEM((nb, lw), F32),
            pltpu.VMEM((cw, lw), F32),
            pltpu.SemaphoreType.DMA((rows_dev // nb,)),
            pltpu.SemaphoreType.DMA((rows_dev // nb,)),
            pltpu.SemaphoreType.DMA,
        ],
        cost_estimate=pl.CostEstimate(flops=2 * 10**9, bytes_accessed=12 * 10**6, transcendentals=0),
        name="final",
    )(pos, owned_list, tab, look_cols, fac_hi, fac_lo, lower_inv, target, *picks, *spread, panel_out)
    return panel_out.T, updated, sketch_t.T


def solution(mesh):
    placed = (P("row", "col"), P("row", "col"), P(None, "row"), P(), P(), P())
    return jax.shard_map(
        functools.partial(on_device, mesh.shape["row"], mesh.shape["col"]),
        mesh=mesh,
        in_specs=placed,
        out_specs=(P("row", "col"), P("row", "col"), P(None, "col")),
        check_vma=False,
    )
```

```python
import functools

import jax
import jax.numpy as jnp
from jax import lax
from jax.experimental import pallas as pl
from jax.experimental.pallas import tpu as pltpu
from jax.sharding import PartitionSpec as P


F32, BF16, I32 = jnp.float32, jnp.bfloat16, jnp.int32
GROUP = 4
GROUP_ROWS = 8
PICK_VMEM = 54_000_000
VMEM = pl.BlockSpec(memory_space=pltpu.VMEM)
SMEM = pl.BlockSpec(memory_space=pltpu.SMEM)
HBM = pl.BlockSpec(memory_space=pl.ANY)
FAR = pl.BlockSpec(memory_space=pltpu.HBM)


def split2(x):
    hi = x.astype(BF16)
    return hi, (x - hi.astype(F32)).astype(BF16)


def split3(x):
    hi = x.astype(BF16)
    rest = x - hi.astype(F32)
    mid = rest.astype(BF16)
    return hi, mid, (rest - mid.astype(F32)).astype(BF16)


def mm(a, b, dims=((1,), (0,))):
    return lax.dot_general(a, b, (dims, ((), ())), preferred_element_type=F32)


def mm3(a, b, dims=((1,), (0,))):
    return mm(a[0], b[0], dims) + (mm(a[0], b[1], dims) + mm(a[1], b[0], dims))


def pick_kernel(pivots, look, panel, sketch_map, pivot_row, *rest):
    outs, (head, pan, ske, extra, sem, in_sem) = rest[:GROUP], rest[GROUP:]
    slots = pivot_row.shape[1]
    rows_dev = panel.shape[1]
    chunk = slots // GROUP
    extra_rows = extra.shape[0] // GROUP
    split = sketch_map.shape[0]
    step = rows_dev // GROUP
    row = lax.axis_index("row")
    q = lax.rem(row, GROUP)
    first = row * rows_dev

    def loads(k):
        part = pl.ds(k * step, step)
        return (
            pltpu.make_async_copy(panel.at[:, part], pan.at[:, part], in_sem.at[k]),
            pltpu.make_async_copy(sketch_map.at[:, part], ske.at[:, part], in_sem.at[GROUP + k]),
        )

    for k in range(GROUP):
        for copy in loads(k):
            copy.start()
    target = pivot_row[...] - first
    sketch_sum = jnp.zeros((panel.shape[0], split), F32)
    pick_sum = jnp.zeros((panel.shape[0], slots), F32)
    for s in range(GROUP):
        base = (q ^ s) * chunk
        for i in range(chunk):
            there = pivots[base + i] - first
            owned = there.astype(jnp.uint32) < jnp.uint32(rows_dev)
            pltpu.make_async_copy(
                look.at[pl.ds(jnp.where(owned, there, base + i), 1), :],
                outs[s].at[pl.ds(i, 1), :],
                sem.at[s],
            ).start()
        for copy in loads(s):
            copy.wait()
        k = s * step
        hi, mid, lo = split3(pan[:, k : k + step])
        sketch_sum += mm3((hi, mid), split2(ske[:, k : k + step]), ((1,), (1,)))
        hot = one_hot(target, k, step)
        pick_sum += (mm(hi, hot) + mm(mid, hot)) + mm(lo, hot)
    head[...] = pan[:, :slots]
    extra[:, :split] = sketch_sum
    extra[:, split:] = pick_sum
    for s in range(GROUP):
        rows = pl.ds(pl.multiple_of((q ^ s) * extra_rows, 8), extra_rows)
        outs[s][chunk : chunk + extra_rows, :] = extra[rows, :]
    for s in range(GROUP):
        pltpu.make_async_copy(
            look.at[pl.ds(0, chunk), :], outs[s].at[pl.ds(0, chunk), :], sem.at[s]
        ).wait()


def list_kernel(pivots, owned_list, *, rows_dev):
    slots = pivots.shape[0]
    wide = slots + GROUP_ROWS
    first = lax.axis_index("row") * rows_dev

    def note(p, count):
        there = pivots[p] - first
        owned_list[count] = p
        owned_list[wide + count] = there
        return count + (there.astype(jnp.uint32) < jnp.uint32(rows_dev)).astype(I32)

    count = lax.fori_loop(0, slots, note, jnp.int32(0), unroll=64)
    last = jnp.maximum(count - 1, 0)
    for i in range(GROUP_ROWS):
        owned_list[count + i] = owned_list[last]
        owned_list[wide + count + i] = owned_list[wide + last]
    owned_list[2 * wide] = count


def one_hot(target, k, step):
    place = lax.broadcasted_iota(I32, (step, target.shape[1]), 0) + k
    return jnp.where(place == target, 1.0, 0.0).astype(BF16)


def place_rows(owned_list, slots, source, out):
    count = owned_list[2 * (slots + GROUP_ROWS)]

    @pl.loop(0, pl.cdiv(count, GROUP_ROWS))
    def _(k):
        rows = [
            source[pl.ds(owned_list[k * GROUP_ROWS + i], 1), :] for i in range(GROUP_ROWS)
        ]
        for i in range(GROUP_ROWS):
            out[pl.ds(owned_list[slots + GROUP_ROWS + k * GROUP_ROWS + i], 1), :] = rows[i]


def triangle(upper):
    shape = upper.shape
    keep = lax.broadcasted_iota(I32, shape, 0) <= lax.broadcasted_iota(I32, shape, 1)
    return split2(jnp.where(keep, upper[...], 0.0))


def factor_kernel(order, *rest):
    blocks, (upper, upper_own, fac_hi, fac_lo, own_out, whole) = rest[:-6], rest[-6:]
    cw, rows_dev = blocks[0].shape
    nb = upper.shape[0]
    col = lax.axis_index("col")
    tri = triangle(upper)
    own = split2(upper_own[...])
    for b in range(rows_dev // nb):
        lanes = pl.ds(b * nb, nb)
        for k, block in zip(order, blocks):
            rows = pl.ds(pl.multiple_of((col ^ k) * cw, 8), cw)
            whole[b % 2, rows, :] = block[:, lanes]
        data = whole[b % 2]
        fac_hi[lanes, :], fac_lo[lanes, :] = split2(mm3(split2(data.T), tri))
        own_out[:, lanes] = mm3(own, split2(data))


def head_kernel(order, pivot_row, *rest):
    heads, (upper, upper_own, hi_in, lo_in, own_in, fac_hi, fac_lo, own_out, top) = rest[:-9], rest[-9:]
    cw, rows_dev = own_in.shape
    nb = upper.shape[0]
    col = lax.axis_index("col")
    for k, head in zip(order, heads):
        top[pl.ds(pl.multiple_of((col ^ k) * cw, 8), cw), :] = head[...]
    data = top[...]
    hi, lo = split2(mm3(split2(data.T), triangle(upper)))
    lanes = 128
    right = jnp.concatenate([hi, lo, jnp.ones((nb, lanes), BF16)], axis=1)
    parts = split3(mm3(split2(upper_own[...]), split2(data)))
    left = jnp.concatenate([*parts, jnp.ones((16, nb), BF16)])
    first = lax.axis_index("row") * rows_dev
    for b in range(rows_dev // nb):
        part = pl.ds(b * nb, nb)
        hot = one_hot(pivot_row[...] - first, b * nb, nb)
        moved = mm(left, hot, ((1,), (1,)))
        new = (moved[:cw] + moved[cw : 2 * cw]) + moved[2 * cw : 3 * cw]
        own_out[:, part] = jnp.where(moved[3 * cw : 3 * cw + 1] > 0.5, new, own_in[:, part])
        moved = mm(hot, right)
        hit = jnp.concatenate([moved[:, 2 * nb :]] * (nb // lanes), axis=1) > 0.5
        fac_hi[part, :] = jnp.where(hit, moved[:, :nb], hi_in[part, :].astype(F32)).astype(BF16)
        fac_lo[part, :] = jnp.where(hit, moved[:, nb : 2 * nb], lo_in[part, :].astype(F32)).astype(BF16)


def final_kernel(owned_list, look, fac_hi, fac_lo, lower, target, *rest):
    picks, spread = rest[:GROUP], rest[GROUP : 2 * GROUP]
    _, updated, panel_out, sketch_out, buf, piv, got, extra, in_sem, out_sem, top_sem = rest[2 * GROUP :]
    row = lax.axis_index("row")
    q = lax.rem(row, GROUP)
    slots = target.shape[0]
    chunk = slots // GROUP
    rows_dev = buf.shape[0]
    extra_rows = extra.shape[0] // GROUP
    blocks = rows_dev // slots

    def load(b):
        part = pl.ds(b * slots, slots)
        return pltpu.make_async_copy(look.at[part, :], buf.at[part, :], in_sem.at[b])

    def store(b):
        part = pl.ds(b * slots, slots)
        return pltpu.make_async_copy(buf.at[part, :], updated.at[part, :], out_sem.at[b])

    for b in range(blocks):
        load(b).start()
    for s in range(GROUP):
        part = pl.ds(pl.multiple_of((q ^ s) * chunk, 8), chunk)
        mine = target[part, :] >= 0
        there = spread[s][:chunk, :]
        piv[part, :] = jnp.where(mine, picks[s][:chunk, :], there)
        got[part, :] = there
        erows = pl.ds(pl.multiple_of((q ^ s) * extra_rows, 8), extra_rows)
        extra[erows, :] = spread[s][chunk : chunk + extra_rows, :]
    split = sketch_out.shape[1]
    sketch_out[...] = extra[:, :split]

    below = lax.broadcasted_iota(I32, (slots, slots), 0) > lax.broadcasted_iota(I32, (slots, slots), 1)
    low = split2(jnp.where(below, lower[...], 0.0))
    first = piv[...]
    u_rows = first + mm3(low, split2(first))
    u_hi, u_lo = split2(u_rows)

    for b in range(blocks):
        load(b).wait()

    @pl.when(row == 0)
    def _():
        place_rows(owned_list, slots, buf, buf)

    @pl.when(row != 0)
    def _():
        place_rows(owned_list, slots, got, buf)

    for b in range(blocks):
        part = pl.ds(b * slots, slots)
        drop = mm3((fac_hi[part, :], fac_lo[part, :]), (u_hi, u_lo))
        new = buf[part, :] - drop
        if b == 0:
            new = jnp.where(row == 0, u_rows, new)
        buf[part, :] = new
        store(b).start()

    top = pltpu.make_async_copy(
        extra.at[:, pl.ds(split, slots)], panel_out.at[:, pl.ds(0, slots)], top_sem
    )

    @pl.when(row == 0)
    def _():
        top.start()
        top.wait()

    for b in range(blocks):
        store(b).wait()


def on_device(n_row, n_col, panel_col, look_cols, sketch_map, upper_inv, lower_inv, pivots):
    rows_dev, cw = panel_col.shape
    lw = look_cols.shape[1]
    nb, ks = upper_inv.shape[0], sketch_map.shape[0]
    chunk, extra_rows = nb // GROUP, cw // GROUP
    assert ks + nb == lw and n_row % GROUP == 0
    assert n_row & (n_row - 1) == 0 and n_col & (n_col - 1) == 0
    row, col = lax.axis_index("row"), lax.axis_index("col")
    q = row % GROUP
    panel_t = panel_col.T
    owner = pivots // rows_dev
    local = pivots - row * rows_dev
    pivot_row = pivots.reshape(1, nb)
    target = jnp.where(owner == row, local, -1)[:, None]

    def across(v, s):
        return lax.ppermute(v, "row", [(i, i ^ s) for i in range(n_row)])

    message = jax.ShapeDtypeStruct((chunk + extra_rows, lw), F32)
    *picks, head = pl.pallas_call(
        pick_kernel,
        out_shape=[message] * GROUP
        + [jax.ShapeDtypeStruct((cw, nb), F32)],
        in_specs=[SMEM, FAR, FAR, FAR, VMEM],
        out_specs=[VMEM] * (GROUP + 1),
        scratch_shapes=[
            pltpu.VMEM((cw, rows_dev), F32),
            pltpu.VMEM((ks, rows_dev), F32),
            pltpu.VMEM((cw, lw), F32),
            pltpu.SemaphoreType.DMA((GROUP,)),
            pltpu.SemaphoreType.DMA((2 * GROUP,)),
        ],
        cost_estimate=pl.CostEstimate(flops=10**9, bytes_accessed=4 * 10**6, transcendentals=0),
        compiler_params=pltpu.CompilerParams(vmem_limit_bytes=PICK_VMEM),
        name="pick",
    )(pivots, look_cols, panel_t, sketch_map, pivot_row)
    owned_list = pl.pallas_call(
        functools.partial(list_kernel, rows_dev=rows_dev),
        out_shape=jax.ShapeDtypeStruct((2 * (nb + GROUP_ROWS) + 8,), I32),
        in_specs=[SMEM],
        out_specs=SMEM,
        cost_estimate=pl.CostEstimate(flops=10**8, bytes_accessed=10**6, transcendentals=0),
        name="list",
    )(pivots)

    slot_owner = lax.dynamic_slice_in_dim(owner, q * chunk, chunk)
    slot_owner = jnp.concatenate([slot_owner, jnp.full((extra_rows,), -1, I32)])[:, None]
    summed = slot_owner < 0
    got = [picks[0]] + [across(picks[s], s) for s in range(1, GROUP)]
    have = sum(jnp.where(summed | (slot_owner == (row ^ s)), got[s], 0.0) for s in range(GROUP))
    top = got[0]
    for s in range(1, GROUP):
        top = jnp.where(row == s, got[s], top)
    bit = GROUP
    while bit < n_row:
        inside = summed | (slot_owner // bit == row // bit)
        got = across(jnp.where(inside, have, top), bit)
        other = (row // bit) ^ 1
        theirs = slot_owner // bit == other
        have = jnp.where(theirs, 0.0, have) + jnp.where(summed | theirs, got, 0.0)
        top = jnp.where(other == 0, got, top)
        bit *= 2
    spread = [jnp.where(slot_owner == (row ^ s), top, have) for s in range(GROUP)]
    spread = spread[:1] + [across(spread[s], s) for s in range(1, GROUP)]

    blocks = {0: panel_t}
    bit = n_col // 2
    while bit:
        for k in list(blocks):
            pairs = [(i, i ^ bit) for i in range(n_col)]
            blocks[k ^ bit] = lax.ppermute(blocks[k], "col", pairs)
        bit //= 2
    bit = 1
    while bit < n_row:
        sent = lax.ppermute(head, "row", [(i, i + bit) for i in range(bit)])
        head = jnp.where(row // bit == 1, sent, head)
        bit *= 2
    heads = {0: head}
    bit = n_col // 2
    while bit:
        pairs = [(i, i ^ bit) for i in range(n_col)]
        for k in list(heads):
            heads[k ^ bit] = lax.ppermute(heads[k], "col", pairs)
        bit //= 2
    order = list(heads)
    blocks = [blocks[k] for k in order]
    upper_own = lax.dynamic_slice_in_dim(jnp.triu(upper_inv), col * cw, cw, 1).T

    split_factor = [jax.ShapeDtypeStruct((rows_dev, nb), BF16)] * 2
    own_shape = jax.ShapeDtypeStruct((cw, rows_dev), F32)
    *raw, own_raw = pl.pallas_call(
        functools.partial(factor_kernel, order),
        out_shape=[*split_factor, own_shape],
        in_specs=[VMEM] * (n_col + 2),
        out_specs=[VMEM] * 3,
        scratch_shapes=[pltpu.VMEM((2, nb, nb), F32)],
        cost_estimate=pl.CostEstimate(flops=10**9, bytes_accessed=4 * 10**6, transcendentals=0),
        compiler_params=pltpu.CompilerParams(vmem_limit_bytes=12 << 20),
        name="factor",
    )(*blocks, upper_inv, upper_own)
    fac_hi, fac_lo, panel_out = pl.pallas_call(
        functools.partial(head_kernel, order),
        out_shape=[*split_factor, own_shape],
        in_specs=[VMEM] * (6 + n_col),
        out_specs=[VMEM] * 3,
        scratch_shapes=[pltpu.VMEM((nb, nb), F32)],
        cost_estimate=pl.CostEstimate(flops=10**9, bytes_accessed=4 * 10**6, transcendentals=0),
        compiler_params=pltpu.CompilerParams(vmem_limit_bytes=12 << 20),
        name="headfix",
    )(pivot_row, *heads.values(), upper_inv, upper_own, *raw, own_raw)

    n_in = 6 + 2 * GROUP
    updated, panel_out, sketch_t = pl.pallas_call(
        final_kernel,
        out_shape=[
            jax.ShapeDtypeStruct((rows_dev, lw), F32),
            jax.ShapeDtypeStruct((cw, rows_dev), F32),
            jax.ShapeDtypeStruct((cw, ks), F32),
        ],
        in_specs=[SMEM, HBM] + [VMEM] * (4 + 2 * GROUP) + [HBM],
        out_specs=[HBM, HBM, VMEM],
        input_output_aliases={n_in: 1},
        scratch_shapes=[
            pltpu.VMEM((rows_dev, lw), F32),
            pltpu.VMEM((nb, lw), F32),
            pltpu.VMEM((nb, lw), F32),
            pltpu.VMEM((cw, lw), F32),
            pltpu.SemaphoreType.DMA((rows_dev // nb,)),
            pltpu.SemaphoreType.DMA((rows_dev // nb,)),
            pltpu.SemaphoreType.DMA,
        ],
        cost_estimate=pl.CostEstimate(flops=2 * 10**9, bytes_accessed=12 * 10**6, transcendentals=0),
        compiler_params=pltpu.CompilerParams(vmem_limit_bytes=20 << 20),
        name="final",
    )(owned_list, look_cols, fac_hi, fac_lo, lower_inv, target, *picks, *spread, panel_out)
    return panel_out.T, updated, sketch_t.T


def solution(mesh):
    n_row, n_col = mesh.shape["row"], mesh.shape["col"]
    placed = (P("row", "col"), P("row", "col"), P(None, "row"), P(), P(), P())

    def step(*args):
        return on_device(n_row, n_col, *args)

    return jax.shard_map(
        step,
        mesh=mesh,
        in_specs=placed,
        out_specs=(P("row", "col"), P("row", "col"), P(None, "col")),
        check_vma=False,
    )
```

```python
import functools

import jax
import jax.numpy as jnp
from jax import lax
from jax.experimental import pallas as pl
from jax.experimental.pallas import tpu as pltpu
from jax.sharding import PartitionSpec as P


F32, BF16, I32 = jnp.float32, jnp.bfloat16, jnp.int32
GROUP = 4
GROUP_ROWS = 8
PICK_VMEM = 54_000_000
FACTOR_VMEM = 12_000_000
FINAL_VMEM = 20_000_000
VMEM = pl.BlockSpec(memory_space=pltpu.VMEM)
SMEM = pl.BlockSpec(memory_space=pltpu.SMEM)
HBM = pl.BlockSpec(memory_space=pl.ANY)
FAR = pl.BlockSpec(memory_space=pltpu.HBM)


def split2(x):
    hi = x.astype(BF16)
    return hi, (x - hi.astype(F32)).astype(BF16)


def split3(x):
    hi = x.astype(BF16)
    rest = x - hi.astype(F32)
    mid = rest.astype(BF16)
    return hi, mid, (rest - mid.astype(F32)).astype(BF16)


def mm(a, b, dims=((1,), (0,))):
    return lax.dot_general(a, b, (dims, ((), ())), preferred_element_type=F32)


def mm3(a, b, dims=((1,), (0,))):
    return mm(a[0], b[0], dims) + (mm(a[0], b[1], dims) + mm(a[1], b[0], dims))


def pick_kernel(pivots, look, panel, sketch_map, pivot_row, *rest):
    outs, (head, pan, ske, extra, sem, in_sem) = rest[:GROUP], rest[GROUP:]
    slots = pivot_row.shape[1]
    rows_dev = panel.shape[1]
    chunk = slots // GROUP
    extra_rows = extra.shape[0] // GROUP
    split = sketch_map.shape[0]
    step = rows_dev // GROUP
    row = lax.axis_index("row")
    q = lax.rem(row, GROUP)
    first = row * rows_dev

    def loads(k):
        part = pl.ds(k * step, step)
        return (
            pltpu.make_async_copy(panel.at[:, part], pan.at[:, part], in_sem.at[k]),
            pltpu.make_async_copy(sketch_map.at[:, part], ske.at[:, part], in_sem.at[GROUP + k]),
        )

    for k in range(GROUP):
        for copy in loads(k):
            copy.start()
    target = pivot_row[...] - first
    sketch_sum = jnp.zeros((panel.shape[0], split), F32)
    pick_sum = jnp.zeros((panel.shape[0], slots), F32)
    for s in range(GROUP):
        base = (q ^ s) * chunk
        for i in range(chunk):
            there = pivots[base + i] - first
            owned = there.astype(jnp.uint32) < jnp.uint32(rows_dev)
            pltpu.make_async_copy(
                look.at[pl.ds(jnp.where(owned, there, base + i), 1), :],
                outs[s].at[pl.ds(i, 1), :],
                sem.at[s],
            ).start()
        for copy in loads(s):
            copy.wait()
        k = s * step
        hi, mid, lo = split3(pan[:, k : k + step])
        sketch_sum += mm3((hi, mid), split2(ske[:, k : k + step]), ((1,), (1,)))
        hot = one_hot(target, k, step)
        pick_sum += (mm(hi, hot) + mm(mid, hot)) + mm(lo, hot)
    head[...] = pan[:, :slots]
    extra[:, :split] = sketch_sum
    extra[:, split:] = pick_sum
    for s in range(GROUP):
        rows = pl.ds(pl.multiple_of((q ^ s) * extra_rows, 8), extra_rows)
        outs[s][chunk : chunk + extra_rows, :] = extra[rows, :]
    for s in range(GROUP):
        pltpu.make_async_copy(
            look.at[pl.ds(0, chunk), :], outs[s].at[pl.ds(0, chunk), :], sem.at[s]
        ).wait()


def list_kernel(pivots, owned_list, *, rows_dev):
    slots = pivots.shape[0]
    wide = slots + GROUP_ROWS
    first = lax.axis_index("row") * rows_dev

    def note(p, count):
        there = pivots[p] - first
        owned_list[count] = p
        owned_list[wide + count] = there
        return count + (there.astype(jnp.uint32) < jnp.uint32(rows_dev)).astype(I32)

    count = lax.fori_loop(0, slots, note, jnp.int32(0), unroll=64)
    last = jnp.maximum(count - 1, 0)
    for i in range(GROUP_ROWS):
        owned_list[count + i] = owned_list[last]
        owned_list[wide + count + i] = owned_list[wide + last]
    owned_list[2 * wide] = count


def one_hot(target, k, step):
    place = lax.broadcasted_iota(I32, (step, target.shape[1]), 0) + k
    return jnp.where(place == target, 1.0, 0.0).astype(BF16)


def place_rows(owned_list, slots, source, out):
    count = owned_list[2 * (slots + GROUP_ROWS)]

    @pl.loop(0, pl.cdiv(count, GROUP_ROWS))
    def _(k):
        rows = [
            source[pl.ds(owned_list[k * GROUP_ROWS + i], 1), :] for i in range(GROUP_ROWS)
        ]
        for i in range(GROUP_ROWS):
            out[pl.ds(owned_list[slots + GROUP_ROWS + k * GROUP_ROWS + i], 1), :] = rows[i]


def triangle(upper):
    shape = upper.shape
    keep = lax.broadcasted_iota(I32, shape, 0) <= lax.broadcasted_iota(I32, shape, 1)
    return split2(jnp.where(keep, upper[...], 0.0))


def factor_kernel(order, *rest):
    blocks, (upper, fac_hi, fac_lo, whole) = rest[: len(order)], rest[len(order) :]
    cw, rows_dev = blocks[0].shape
    nb = upper.shape[0]
    col = lax.axis_index("col")
    tri = triangle(upper)
    for b in range(rows_dev // nb):
        lanes = pl.ds(b * nb, nb)
        for k, block in zip(order, blocks):
            whole[b % 2, pl.ds(pl.multiple_of((col ^ k) * cw, 8), cw), :] = block[:, lanes]
        fac_hi[lanes, :], fac_lo[lanes, :] = split2(mm3(split2(whole[b % 2].T), tri))


def head_kernel(order, pivot_row, *rest):
    heads, (upper, hi_in, lo_in, fac_hi, fac_lo, own_out, top) = rest[: len(order)], rest[len(order) :]
    cw, rows_dev = own_out.shape
    nb = upper.shape[0]
    col = lax.axis_index("col")
    for k, head in zip(order, heads):
        top[pl.ds(pl.multiple_of((col ^ k) * cw, 8), cw), :] = head[...]
    hi, lo = split2(mm3(split2(top[...].T), triangle(upper)))
    lanes = 128
    right = jnp.concatenate([hi, lo, jnp.ones((nb, lanes), BF16)], axis=1)
    place = lax.broadcasted_iota(I32, (cw, nb), 1) - lax.broadcasted_iota(I32, (cw, nb), 0)
    mine = jnp.where(place == col * cw, 1.0, 0.0).astype(BF16)
    target = pivot_row[...] - lax.axis_index("row") * rows_dev
    nt = ((1,), (1,))
    for b in range(rows_dev // nb):
        part = pl.ds(b * nb, nb)
        moved = mm(one_hot(target, b * nb, nb), right)
        hit = jnp.concatenate([moved[:, 2 * nb :]] * (nb // lanes), axis=1) > 0.5
        hi = jnp.where(hit, moved[:, :nb], hi_in[part, :].astype(F32)).astype(BF16)
        lo = jnp.where(hit, moved[:, nb : 2 * nb], lo_in[part, :].astype(F32)).astype(BF16)
        fac_hi[part, :] = hi
        fac_lo[part, :] = lo
        own_out[:, part] = mm(mine, hi, nt) + mm(mine, lo, nt)


def final_kernel(owned_list, look, fac_hi, fac_lo, lower, pivot_row, *rest):
    picks, spread = rest[:GROUP], rest[GROUP : 2 * GROUP]
    _, updated, panel_out, sketch_out, buf, piv, got, extra, column, in_sem, out_sem, top_sem = rest[2 * GROUP :]
    row = lax.axis_index("row")
    q = lax.rem(row, GROUP)
    slots = pivot_row.shape[1]
    chunk = slots // GROUP
    rows_dev = buf.shape[0]
    extra_rows = extra.shape[0] // GROUP
    blocks = rows_dev // slots

    def load(b):
        part = pl.ds(b * slots, slots)
        return pltpu.make_async_copy(look.at[part, :], buf.at[part, :], in_sem.at[b])

    def store(b):
        part = pl.ds(b * slots, slots)
        return pltpu.make_async_copy(buf.at[part, :], updated.at[part, :], out_sem.at[b])

    for b in range(blocks):
        load(b).start()
    there = pivot_row[...] - row * rows_dev
    here = jnp.where((there >= 0) & (there < rows_dev), 1.0, 0.0)
    column[...] = jnp.broadcast_to(here, (128, slots)).T
    for s in range(GROUP):
        part = pl.ds(pl.multiple_of((q ^ s) * chunk, 8), chunk)
        mine = column[part, :1] > 0.5
        there = spread[s][:chunk, :]
        piv[part, :] = jnp.where(mine, picks[s][:chunk, :], there)
        got[part, :] = there
        erows = pl.ds(pl.multiple_of((q ^ s) * extra_rows, 8), extra_rows)
        extra[erows, :] = spread[s][chunk : chunk + extra_rows, :]
    split = sketch_out.shape[1]
    sketch_out[...] = extra[:, :split]

    below = lax.broadcasted_iota(I32, (slots, slots), 0) > lax.broadcasted_iota(I32, (slots, slots), 1)
    low = split2(jnp.where(below, lower[...], 0.0))
    first = piv[...]
    u_rows = first + mm3(low, split2(first))
    u_hi, u_lo = split2(u_rows)

    for b in range(blocks):
        load(b).wait()

    @pl.when(row == 0)
    def _():
        place_rows(owned_list, slots, buf, buf)

    @pl.when(row != 0)
    def _():
        place_rows(owned_list, slots, got, buf)

    for b in range(blocks):
        part = pl.ds(b * slots, slots)
        drop = mm3((fac_hi[part, :], fac_lo[part, :]), (u_hi, u_lo))
        new = buf[part, :] - drop
        if b == 0:
            new = jnp.where(row == 0, u_rows, new)
        buf[part, :] = new
        store(b).start()

    top = pltpu.make_async_copy(
        extra.at[:, pl.ds(split, slots)], panel_out.at[:, pl.ds(0, slots)], top_sem
    )

    @pl.when(row == 0)
    def _():
        top.start()
        top.wait()

    for b in range(blocks):
        store(b).wait()


def on_device(n_row, n_col, panel_col, look_cols, sketch_map, upper_inv, lower_inv, pivots):
    rows_dev, cw = panel_col.shape
    lw = look_cols.shape[1]
    nb, ks = upper_inv.shape[0], sketch_map.shape[0]
    chunk, extra_rows = nb // GROUP, cw // GROUP
    assert ks + nb == lw and n_row % GROUP == 0
    assert n_row & (n_row - 1) == 0 and n_col & (n_col - 1) == 0
    row = lax.axis_index("row")
    q = row % GROUP
    panel_t = panel_col.T
    owner = pivots // rows_dev
    pivot_row = pivots.reshape(1, nb)

    def across(v, s):
        return lax.ppermute(v, "row", [(i, i ^ s) for i in range(n_row)])

    message = jax.ShapeDtypeStruct((chunk + extra_rows, lw), F32)
    *picks, head = pl.pallas_call(
        pick_kernel,
        out_shape=[message] * GROUP
        + [jax.ShapeDtypeStruct((cw, nb), F32)],
        in_specs=[SMEM, FAR, FAR, FAR, VMEM],
        out_specs=[VMEM] * (GROUP + 1),
        scratch_shapes=[
            pltpu.VMEM((cw, rows_dev), F32),
            pltpu.VMEM((ks, rows_dev), F32),
            pltpu.VMEM((cw, lw), F32),
            pltpu.SemaphoreType.DMA((GROUP,)),
            pltpu.SemaphoreType.DMA((2 * GROUP,)),
        ],
        cost_estimate=pl.CostEstimate(flops=10**9, bytes_accessed=4 * 10**6, transcendentals=0),
        compiler_params=pltpu.CompilerParams(vmem_limit_bytes=PICK_VMEM),
        name="pick",
    )(pivots, look_cols, panel_t, sketch_map, pivot_row)
    owned_list = pl.pallas_call(
        functools.partial(list_kernel, rows_dev=rows_dev),
        out_shape=jax.ShapeDtypeStruct((2 * (nb + GROUP_ROWS) + 8,), I32),
        in_specs=[SMEM],
        out_specs=SMEM,
        cost_estimate=pl.CostEstimate(flops=10**8, bytes_accessed=10**6, transcendentals=0),
        name="list",
    )(pivots)

    slot_owner = lax.dynamic_slice_in_dim(owner, q * chunk, chunk)
    slot_owner = jnp.concatenate([slot_owner, jnp.full((extra_rows,), -1, I32)])[:, None]
    summed = slot_owner < 0
    got = [picks[0]] + [across(picks[s], s) for s in range(1, GROUP)]
    have = sum(jnp.where(summed | (slot_owner == (row ^ s)), got[s], 0.0) for s in range(GROUP))
    top = got[0]
    for s in range(1, GROUP):
        top = jnp.where(row == s, got[s], top)
    bit = GROUP
    while bit < n_row:
        inside = summed | (slot_owner // bit == row // bit)
        got = across(jnp.where(inside, have, top), bit)
        other = (row // bit) ^ 1
        theirs = slot_owner // bit == other
        have = jnp.where(theirs, 0.0, have) + jnp.where(summed | theirs, got, 0.0)
        top = jnp.where(other == 0, got, top)
        bit *= 2
    spread = [jnp.where(slot_owner == (row ^ s), top, have) for s in range(GROUP)]
    spread = spread[:1] + [across(spread[s], s) for s in range(1, GROUP)]

    blocks = {0: panel_t}
    bit = n_col // 2
    while bit:
        for k in list(blocks):
            pairs = [(i, i ^ bit) for i in range(n_col)]
            blocks[k ^ bit] = lax.ppermute(blocks[k], "col", pairs)
        bit //= 2
    bit = 1
    while bit < n_row:
        sent = lax.ppermute(head, "row", [(i, i + bit) for i in range(bit)])
        head = jnp.where(row // bit == 1, sent, head)
        bit *= 2
    heads = {0: head}
    bit = n_col // 2
    while bit:
        pairs = [(i, i ^ bit) for i in range(n_col)]
        for k in list(heads):
            heads[k ^ bit] = lax.ppermute(heads[k], "col", pairs)
        bit //= 2
    order = list(heads)
    blocks = [blocks[k] for k in order]
    split_factor = [jax.ShapeDtypeStruct((rows_dev, nb), BF16)] * 2
    raw = pl.pallas_call(
        functools.partial(factor_kernel, order),
        out_shape=split_factor,
        in_specs=[VMEM] * (n_col + 1),
        out_specs=[VMEM] * 2,
        scratch_shapes=[pltpu.VMEM((2, nb, nb), F32)],
        cost_estimate=pl.CostEstimate(flops=10**9, bytes_accessed=4 * 10**6, transcendentals=0),
        compiler_params=pltpu.CompilerParams(vmem_limit_bytes=FACTOR_VMEM),
        name="factor",
    )(*blocks, upper_inv)
    fac_hi, fac_lo, panel_out = pl.pallas_call(
        functools.partial(head_kernel, order),
        out_shape=[*split_factor, jax.ShapeDtypeStruct((cw, rows_dev), F32)],
        in_specs=[VMEM] * (4 + n_col),
        out_specs=[VMEM] * 3,
        scratch_shapes=[pltpu.VMEM((nb, nb), F32)],
        cost_estimate=pl.CostEstimate(flops=10**9, bytes_accessed=4 * 10**6, transcendentals=0),
        compiler_params=pltpu.CompilerParams(vmem_limit_bytes=FACTOR_VMEM),
        name="headfix",
    )(pivot_row, *heads.values(), upper_inv, *raw)

    n_in = 6 + 2 * GROUP
    updated, panel_out, sketch_t = pl.pallas_call(
        final_kernel,
        out_shape=[
            jax.ShapeDtypeStruct((rows_dev, lw), F32),
            jax.ShapeDtypeStruct((cw, rows_dev), F32),
            jax.ShapeDtypeStruct((cw, ks), F32),
        ],
        in_specs=[SMEM, HBM] + [VMEM] * (4 + 2 * GROUP) + [HBM],
        out_specs=[HBM, HBM, VMEM],
        input_output_aliases={n_in: 1},
        scratch_shapes=[
            pltpu.VMEM((rows_dev, lw), F32),
            pltpu.VMEM((nb, lw), F32),
            pltpu.VMEM((nb, lw), F32),
            pltpu.VMEM((cw, lw), F32),
            pltpu.VMEM((nb, 128), F32),
            pltpu.SemaphoreType.DMA((rows_dev // nb,)),
            pltpu.SemaphoreType.DMA((rows_dev // nb,)),
            pltpu.SemaphoreType.DMA,
        ],
        cost_estimate=pl.CostEstimate(flops=2 * 10**9, bytes_accessed=12 * 10**6, transcendentals=0),
        compiler_params=pltpu.CompilerParams(vmem_limit_bytes=FINAL_VMEM),
        name="final",
    )(owned_list, look_cols, fac_hi, fac_lo, lower_inv, pivot_row, *picks, *spread, panel_out)
    return panel_out.T, updated, sketch_t.T


def solution(mesh):
    n_row, n_col = mesh.shape["row"], mesh.shape["col"]
    placed = (P("row", "col"), P("row", "col"), P(None, "row"), P(), P(), P())

    def step(*args):
        return on_device(n_row, n_col, *args)

    return jax.shard_map(
        step,
        mesh=mesh,
        in_specs=placed,
        out_specs=(P("row", "col"), P("row", "col"), P(None, "col")),
        check_vma=False,
    )
```

```python
import functools

import jax
import jax.numpy as jnp
from jax import lax
from jax.experimental import pallas as pl
from jax.experimental.pallas import tpu as pltpu
from jax.sharding import PartitionSpec as P


F32, BF16, I32 = jnp.float32, jnp.bfloat16, jnp.int32
GROUP = 4
GROUP_ROWS = 8
PICK_VMEM = 54_000_000
FACTOR_VMEM = 12_000_000
FINAL_VMEM = 20_000_000
VMEM = pl.BlockSpec(memory_space=pltpu.VMEM)
SMEM = pl.BlockSpec(memory_space=pltpu.SMEM)
HBM = pl.BlockSpec(memory_space=pl.ANY)
FAR = pl.BlockSpec(memory_space=pltpu.HBM)


def split2(x):
    hi = x.astype(BF16)
    return hi, (x - hi.astype(F32)).astype(BF16)


def split3(x):
    hi = x.astype(BF16)
    rest = x - hi.astype(F32)
    mid = rest.astype(BF16)
    return hi, mid, (rest - mid.astype(F32)).astype(BF16)


def mm(a, b, dims=((1,), (0,))):
    return lax.dot_general(a, b, (dims, ((), ())), preferred_element_type=F32)


def mm3(a, b, dims=((1,), (0,))):
    left = jnp.concatenate([a[0], a[0], a[1]], axis=dims[0][0])
    right = jnp.concatenate([b[0], b[1], b[0]], axis=dims[1][0])
    return mm(left, right, dims)


def pick_kernel(pivots, look, panel, sketch_map, pivot_row, *rest):
    outs, (head, pan, ske, extra, sem, in_sem) = rest[:GROUP], rest[GROUP:]
    slots = pivot_row.shape[1]
    rows_dev = panel.shape[1]
    chunk = slots // GROUP
    extra_rows = extra.shape[0] // GROUP
    split = sketch_map.shape[0]
    step = rows_dev // GROUP
    row = lax.axis_index("row")
    q = lax.rem(row, GROUP)
    first = row * rows_dev

    def loads(k):
        part = pl.ds(k * step, step)
        return (
            pltpu.make_async_copy(panel.at[:, part], pan.at[:, part], in_sem.at[k]),
            pltpu.make_async_copy(sketch_map.at[:, part], ske.at[:, part], in_sem.at[GROUP + k]),
        )

    for k in range(GROUP):
        for copy in loads(k):
            copy.start()
    target = pivot_row[...] - first
    sketch_sum = jnp.zeros((panel.shape[0], split), F32)
    pick_sum = jnp.zeros((panel.shape[0], slots), F32)
    for s in range(GROUP):
        base = (q ^ s) * chunk
        for i in range(chunk):
            there = pivots[base + i] - first
            owned = there.astype(jnp.uint32) < jnp.uint32(rows_dev)
            pltpu.make_async_copy(
                look.at[pl.ds(jnp.where(owned, there, base + i), 1), :],
                outs[s].at[pl.ds(i, 1), :],
                sem.at[s],
            ).start()
        for copy in loads(s):
            copy.wait()
        k = s * step
        hi, mid, lo = split3(pan[:, k : k + step])
        sketch_sum += mm3((hi, mid), split2(ske[:, k : k + step]), ((1,), (1,)))
        hot = one_hot(target, k, step)
        pick_sum += (mm(hi, hot) + mm(mid, hot)) + mm(lo, hot)
    head[...] = pan[:, :slots]
    extra[:, :split] = sketch_sum
    extra[:, split:] = pick_sum
    for s in range(GROUP):
        rows = pl.ds(pl.multiple_of((q ^ s) * extra_rows, 8), extra_rows)
        outs[s][chunk : chunk + extra_rows, :] = extra[rows, :]
    for s in range(GROUP):
        pltpu.make_async_copy(
            look.at[pl.ds(0, chunk), :], outs[s].at[pl.ds(0, chunk), :], sem.at[s]
        ).wait()


def one_hot(target, k, step):
    place = lax.broadcasted_iota(I32, (step, target.shape[1]), 0) + k
    return jnp.where(place == target, 1.0, 0.0).astype(BF16)


def place_rows(owned_list, slots, source, out):
    count = owned_list[2 * (slots + GROUP_ROWS)]

    @pl.loop(0, pl.cdiv(count, GROUP_ROWS))
    def _(k):
        rows = [
            source[pl.ds(owned_list[k * GROUP_ROWS + i], 1), :] for i in range(GROUP_ROWS)
        ]
        for i in range(GROUP_ROWS):
            out[pl.ds(owned_list[slots + GROUP_ROWS + k * GROUP_ROWS + i], 1), :] = rows[i]


def triangle(upper):
    shape = upper.shape
    keep = lax.broadcasted_iota(I32, shape, 0) <= lax.broadcasted_iota(I32, shape, 1)
    return split2(jnp.where(keep, upper[...], 0.0))


def factor_kernel(order, pivots, pivot_row, *rest):
    blocks, (upper, upper_own, fac_hi, fac_lo, own_out, owned_list, whole) = (
        rest[: len(order)],
        rest[len(order) :],
    )
    cw, rows_dev = blocks[0].shape
    nb = upper.shape[0]
    wide = nb + GROUP_ROWS
    col = lax.axis_index("col")
    first = lax.axis_index("row") * rows_dev
    target = pivot_row[...] - first
    tri = triangle(upper)
    own = split2(upper_own[...])
    steps = rows_dev // nb
    count = jnp.int32(0)
    for b in range(steps):
        lanes = pl.ds(b * nb, nb)
        for k, block in zip(order, blocks):
            whole[b % 2, pl.ds(pl.multiple_of((col ^ k) * cw, 8), cw), :] = block[:, lanes]
        for p in range(b * nb // steps, (b + 1) * nb // steps):
            there = pivots[p] - first
            owned_list[count] = p
            owned_list[wide + count] = there
            count = count + (there.astype(jnp.uint32) < jnp.uint32(rows_dev)).astype(I32)
        data = whole[b % 2]
        place = lax.broadcasted_iota(I32, (nb, nb), 0) + b * nb
        hit = jnp.max(jnp.where(place == target, 1.0, 0.0), axis=1, keepdims=True)
        fac = jnp.where(hit > 0.5, 0.0, mm3(split2(data.T), tri))
        fac_hi[lanes, :], fac_lo[lanes, :] = split2(fac)
        own_out[:, lanes] = mm3(own, split2(data))
    last = jnp.maximum(count - 1, 0)
    for i in range(GROUP_ROWS):
        owned_list[count + i] = owned_list[last]
        owned_list[wide + count + i] = owned_list[wide + last]
    owned_list[2 * wide] = count


def head_kernel(order, pivot_row, *rest):
    heads, (upper, upper_own, own_in, top_hi, top_lo, own_out, top) = (
        rest[: len(order)],
        rest[len(order) :],
    )
    cw, rows_dev = own_in.shape
    nb = upper.shape[0]
    col = lax.axis_index("col")
    for k, head in zip(order, heads):
        top[pl.ds(pl.multiple_of((col ^ k) * cw, 8), cw), :] = head[...]
    data = top[...]
    top_hi[...], top_lo[...] = split2(mm3(split2(data.T), triangle(upper)))
    parts = split3(mm3(split2(upper_own[...]), split2(data)))
    left = jnp.concatenate([*parts, jnp.ones((16, nb), BF16)])
    target = pivot_row[...] - lax.axis_index("row") * rows_dev
    for b in range(rows_dev // nb):
        part = pl.ds(b * nb, nb)
        moved = mm(left, one_hot(target, b * nb, nb), ((1,), (1,)))
        new = (moved[:cw] + moved[cw : 2 * cw]) + moved[2 * cw : 3 * cw]
        own_out[:, part] = jnp.where(moved[3 * cw : 3 * cw + 1] > 0.5, new, own_in[:, part])


def final_kernel(owned_list, look, fac_hi, fac_lo, top_hi, top_lo, lower, pivot_row, *rest):
    picks, spread = rest[:GROUP], rest[GROUP : 2 * GROUP]
    _, updated, panel_out, sketch_out, buf, piv, got, extra, column, in_sem, out_sem, top_sem = rest[2 * GROUP :]
    row = lax.axis_index("row")
    q = lax.rem(row, GROUP)
    slots = pivot_row.shape[1]
    chunk = slots // GROUP
    rows_dev = buf.shape[0]
    extra_rows = extra.shape[0] // GROUP
    blocks = rows_dev // slots

    def load(b):
        part = pl.ds(b * slots, slots)
        return pltpu.make_async_copy(look.at[part, :], buf.at[part, :], in_sem.at[b])

    def store(b):
        part = pl.ds(b * slots, slots)
        return pltpu.make_async_copy(buf.at[part, :], updated.at[part, :], out_sem.at[b])

    for b in range(blocks):
        load(b).start()
    there = pivot_row[...] - row * rows_dev
    here = jnp.where((there >= 0) & (there < rows_dev), 1.0, 0.0)
    column[...] = jnp.broadcast_to(here, (128, slots)).T
    for s in range(GROUP):
        part = pl.ds(pl.multiple_of((q ^ s) * chunk, 8), chunk)
        mine = column[part, :1] > 0.5
        there = spread[s][:chunk, :]
        piv[part, :] = jnp.where(mine, picks[s][:chunk, :], there)
        got[part, :] = there
        erows = pl.ds(pl.multiple_of((q ^ s) * extra_rows, 8), extra_rows)
        extra[erows, :] = spread[s][chunk : chunk + extra_rows, :]
    split = sketch_out.shape[1]
    sketch_out[...] = extra[:, :split]

    below = lax.broadcasted_iota(I32, (slots, slots), 0) > lax.broadcasted_iota(I32, (slots, slots), 1)
    low = split2(jnp.where(below, lower[...], 0.0))
    first = piv[...]
    u_rows = first + mm3(low, split2(first))
    u_hi, u_lo = split2(u_rows)

    load(0).wait()
    base = jnp.where(row == 0, buf[:slots, :], got[...])
    got[...] = base - mm3((top_hi[...], top_lo[...]), (u_hi, u_lo))
    for b in range(1, blocks):
        load(b).wait()
    place_rows(owned_list, slots, got, buf)

    for b in range(blocks):
        part = pl.ds(b * slots, slots)
        drop = mm3((fac_hi[part, :], fac_lo[part, :]), (u_hi, u_lo))
        new = buf[part, :] - drop
        if b == 0:
            new = jnp.where(row == 0, u_rows, new)
        buf[part, :] = new
        store(b).start()

    top = pltpu.make_async_copy(
        extra.at[:, pl.ds(split, slots)], panel_out.at[:, pl.ds(0, slots)], top_sem
    )

    @pl.when(row == 0)
    def _():
        top.start()
        top.wait()

    for b in range(blocks):
        store(b).wait()


def on_device(n_row, n_col, panel_col, look_cols, sketch_map, upper_inv, lower_inv, pivots):
    rows_dev, cw = panel_col.shape
    lw = look_cols.shape[1]
    nb, ks = upper_inv.shape[0], sketch_map.shape[0]
    chunk, extra_rows = nb // GROUP, cw // GROUP
    assert ks + nb == lw and n_row % GROUP == 0
    assert n_row & (n_row - 1) == 0 and n_col & (n_col - 1) == 0
    row, col = lax.axis_index("row"), lax.axis_index("col")
    q = row % GROUP
    panel_t = panel_col.T
    owner = pivots // rows_dev
    pivot_row = pivots.reshape(1, nb)

    def across(v, s):
        return lax.ppermute(v, "row", [(i, i ^ s) for i in range(n_row)])

    message = jax.ShapeDtypeStruct((chunk + extra_rows, lw), F32)
    *picks, head = pl.pallas_call(
        pick_kernel,
        out_shape=[message] * GROUP
        + [jax.ShapeDtypeStruct((cw, nb), F32)],
        in_specs=[SMEM, FAR, FAR, FAR, VMEM],
        out_specs=[VMEM] * (GROUP + 1),
        scratch_shapes=[
            pltpu.VMEM((cw, rows_dev), F32),
            pltpu.VMEM((ks, rows_dev), F32),
            pltpu.VMEM((cw, lw), F32),
            pltpu.SemaphoreType.DMA((GROUP,)),
            pltpu.SemaphoreType.DMA((2 * GROUP,)),
        ],
        cost_estimate=pl.CostEstimate(flops=10**9, bytes_accessed=4 * 10**6, transcendentals=0),
        compiler_params=pltpu.CompilerParams(vmem_limit_bytes=PICK_VMEM),
        name="pick",
    )(pivots, look_cols, panel_t, sketch_map, pivot_row)

    slot_owner = lax.dynamic_slice_in_dim(owner, q * chunk, chunk)
    slot_owner = jnp.concatenate([slot_owner, jnp.full((extra_rows,), -1, I32)])[:, None]
    summed = slot_owner < 0
    got = [picks[0]] + [across(picks[s], s) for s in range(1, GROUP)]
    have = sum(jnp.where(summed | (slot_owner == (row ^ s)), got[s], 0.0) for s in range(GROUP))
    top = got[0]
    for s in range(1, GROUP):
        top = jnp.where(row == s, got[s], top)
    bit = GROUP
    while bit < n_row:
        inside = summed | (slot_owner // bit == row // bit)
        got = across(jnp.where(inside, have, top), bit)
        other = (row // bit) ^ 1
        theirs = slot_owner // bit == other
        have = jnp.where(theirs, 0.0, have) + jnp.where(summed | theirs, got, 0.0)
        top = jnp.where(other == 0, got, top)
        bit *= 2
    spread = [jnp.where(slot_owner == (row ^ s), top, have) for s in range(GROUP)]
    spread = spread[:1] + [across(spread[s], s) for s in range(1, GROUP)]

    blocks = {0: panel_t}
    bit = n_col // 2
    while bit:
        for k in list(blocks):
            pairs = [(i, i ^ bit) for i in range(n_col)]
            blocks[k ^ bit] = lax.ppermute(blocks[k], "col", pairs)
        bit //= 2
    bit = 1
    while bit < n_row:
        sent = lax.ppermute(head, "row", [(i, i + bit) for i in range(bit)])
        head = jnp.where(row // bit == 1, sent, head)
        bit *= 2
    heads = {0: head}
    bit = n_col // 2
    while bit:
        pairs = [(i, i ^ bit) for i in range(n_col)]
        for k in list(heads):
            heads[k ^ bit] = lax.ppermute(heads[k], "col", pairs)
        bit //= 2
    order = list(heads)
    blocks = [blocks[k] for k in order]
    upper_own = lax.dynamic_slice_in_dim(jnp.triu(upper_inv), col * cw, cw, 1).T
    own_shape = jax.ShapeDtypeStruct((cw, rows_dev), F32)
    fac_hi, fac_lo, own_raw, owned_list = pl.pallas_call(
        functools.partial(factor_kernel, order),
        out_shape=[jax.ShapeDtypeStruct((rows_dev, nb), BF16)] * 2
        + [own_shape, jax.ShapeDtypeStruct((2 * (nb + GROUP_ROWS) + 8,), I32)],
        in_specs=[SMEM] + [VMEM] * (n_col + 3),
        out_specs=[VMEM] * 3 + [SMEM],
        scratch_shapes=[pltpu.VMEM((2, nb, nb), F32)],
        cost_estimate=pl.CostEstimate(flops=10**9, bytes_accessed=4 * 10**6, transcendentals=0),
        compiler_params=pltpu.CompilerParams(vmem_limit_bytes=FACTOR_VMEM),
        name="factor",
    )(pivots, pivot_row, *blocks, upper_inv, upper_own)
    top_hi, top_lo, panel_out = pl.pallas_call(
        functools.partial(head_kernel, order),
        out_shape=[jax.ShapeDtypeStruct((nb, nb), BF16)] * 2 + [own_shape],
        in_specs=[VMEM] * (4 + n_col),
        out_specs=[VMEM] * 3,
        scratch_shapes=[pltpu.VMEM((nb, nb), F32)],
        cost_estimate=pl.CostEstimate(flops=10**9, bytes_accessed=4 * 10**6, transcendentals=0),
        compiler_params=pltpu.CompilerParams(vmem_limit_bytes=FACTOR_VMEM),
        name="headfix",
    )(pivot_row, *heads.values(), upper_inv, upper_own, own_raw)

    n_in = 8 + 2 * GROUP
    updated, panel_out, sketch_t = pl.pallas_call(
        final_kernel,
        out_shape=[
            jax.ShapeDtypeStruct((rows_dev, lw), F32),
            jax.ShapeDtypeStruct((cw, rows_dev), F32),
            jax.ShapeDtypeStruct((cw, ks), F32),
        ],
        in_specs=[SMEM, HBM] + [VMEM] * (6 + 2 * GROUP) + [HBM],
        out_specs=[HBM, HBM, VMEM],
        input_output_aliases={n_in: 1},
        scratch_shapes=[
            pltpu.VMEM((rows_dev, lw), F32),
            pltpu.VMEM((nb, lw), F32),
            pltpu.VMEM((nb, lw), F32),
            pltpu.VMEM((cw, lw), F32),
            pltpu.VMEM((nb, 128), F32),
            pltpu.SemaphoreType.DMA((rows_dev // nb,)),
            pltpu.SemaphoreType.DMA((rows_dev // nb,)),
            pltpu.SemaphoreType.DMA,
        ],
        cost_estimate=pl.CostEstimate(flops=2 * 10**9, bytes_accessed=12 * 10**6, transcendentals=0),
        compiler_params=pltpu.CompilerParams(vmem_limit_bytes=FINAL_VMEM),
        name="final",
    )(owned_list, look_cols, fac_hi, fac_lo, top_hi, top_lo, lower_inv, pivot_row, *picks, *spread, panel_out)
    return panel_out.T, updated, sketch_t.T


def solution(mesh):
    n_row, n_col = mesh.shape["row"], mesh.shape["col"]
    placed = (P("row", "col"), P("row", "col"), P(None, "row"), P(), P(), P())

    def step(*args):
        return on_device(n_row, n_col, *args)

    return jax.shard_map(
        step,
        mesh=mesh,
        in_specs=placed,
        out_specs=(P("row", "col"), P("row", "col"), P(None, "col")),
        check_vma=False,
    )
```

```python
import functools

import jax
import jax.numpy as jnp
from jax import lax
from jax.experimental import pallas as pl
from jax.experimental.pallas import tpu as pltpu
from jax.sharding import PartitionSpec as P


F32, BF16, I32 = jnp.float32, jnp.bfloat16, jnp.int32
GROUP = 4
GROUP_ROWS = 8
PICK_VMEM = 54_000_000
FACTOR_VMEM = 12_000_000
FINAL_VMEM = 20_000_000
VMEM = pl.BlockSpec(memory_space=pltpu.VMEM)
SMEM = pl.BlockSpec(memory_space=pltpu.SMEM)
HBM = pl.BlockSpec(memory_space=pl.ANY)
FAR = pl.BlockSpec(memory_space=pltpu.HBM)


def split2(x):
    hi = x.astype(BF16)
    return hi, (x - hi.astype(F32)).astype(BF16)


def split3(x):
    hi = x.astype(BF16)
    rest = x - hi.astype(F32)
    mid = rest.astype(BF16)
    return hi, mid, (rest - mid.astype(F32)).astype(BF16)


def mm(a, b, dims=((1,), (0,))):
    return lax.dot_general(a, b, (dims, ((), ())), preferred_element_type=F32)


def mm3(a, b, dims=((1,), (0,))):
    left = jnp.concatenate([a[0], a[0], a[1]], axis=dims[0][0])
    right = jnp.concatenate([b[0], b[1], b[0]], axis=dims[1][0])
    return mm(left, right, dims)


def pick_kernel(pivots, look, panel, sketch_map, pivot_row, *rest):
    outs, (head, pan, ske, extra, sem, in_sem) = rest[:GROUP], rest[GROUP:]
    slots = pivot_row.shape[1]
    rows_dev = panel.shape[1]
    chunk = slots // GROUP
    extra_rows = extra.shape[0] // GROUP
    split = sketch_map.shape[0]
    step = rows_dev // GROUP
    row = lax.axis_index("row")
    q = lax.rem(row, GROUP)
    first = row * rows_dev

    def loads(k):
        part = pl.ds(k * step, step)
        return (
            pltpu.make_async_copy(panel.at[:, part], pan.at[:, part], in_sem.at[k]),
            pltpu.make_async_copy(sketch_map.at[:, part], ske.at[:, part], in_sem.at[GROUP + k]),
        )

    for k in range(GROUP):
        for copy in loads(k):
            copy.start()
    target = pivot_row[...] - first
    sketch_sum = jnp.zeros((panel.shape[0], split), F32)
    pick_sum = jnp.zeros((panel.shape[0], slots), F32)
    for s in range(GROUP):
        base = (q ^ s) * chunk
        for i in range(chunk):
            there = pivots[base + i] - first
            owned = there.astype(jnp.uint32) < jnp.uint32(rows_dev)
            pltpu.make_async_copy(
                look.at[pl.ds(jnp.where(owned, there, base + i), 1), :],
                outs[s].at[pl.ds(i, 1), :],
                sem.at[s],
            ).start()
        for copy in loads(s):
            copy.wait()
        k = s * step
        hi, mid, lo = split3(pan[:, k : k + step])
        sketch_sum += mm3((hi, mid), split2(ske[:, k : k + step]), ((1,), (1,)))
        hot = one_hot(target, k, step)
        pick_sum += (mm(hi, hot) + mm(mid, hot)) + mm(lo, hot)
    head[...] = pan[:, :slots]
    extra[:, :split] = sketch_sum
    extra[:, split:] = pick_sum
    for s in range(GROUP):
        rows = pl.ds(pl.multiple_of((q ^ s) * extra_rows, 8), extra_rows)
        outs[s][chunk : chunk + extra_rows, :] = extra[rows, :]
    for s in range(GROUP):
        pltpu.make_async_copy(
            look.at[pl.ds(0, chunk), :], outs[s].at[pl.ds(0, chunk), :], sem.at[s]
        ).wait()


def one_hot(target, k, step):
    place = lax.broadcasted_iota(I32, (step, target.shape[1]), 0) + k
    return jnp.where(place == target, 1.0, 0.0).astype(BF16)


def place_rows(owned_list, slots, source, out):
    @pl.loop(0, pl.cdiv(owned_list[slots + GROUP_ROWS], GROUP_ROWS))
    def _(k):
        entries = [owned_list[k * GROUP_ROWS + i] for i in range(GROUP_ROWS)]
        rows = [source[pl.ds(entry >> 16, 1), :] for entry in entries]
        for entry, value in zip(entries, rows):
            out[pl.ds(entry & 0xFFFF, 1), :] = value


def triangle(upper):
    shape = upper.shape
    keep = lax.broadcasted_iota(I32, shape, 0) <= lax.broadcasted_iota(I32, shape, 1)
    return split2(jnp.where(keep, upper[...], 0.0))


def factor_kernel(order, pivots, pivot_row, *rest):
    blocks, (upper, upper_own, fac_hi, fac_lo, own_out, owned_list, whole) = (
        rest[: len(order)],
        rest[len(order) :],
    )
    cw, rows_dev = blocks[0].shape
    nb = upper.shape[0]
    wide = nb + GROUP_ROWS
    col = lax.axis_index("col")
    first = lax.axis_index("row") * rows_dev
    target = pivot_row[...] - first
    tri = triangle(upper)
    own = split2(upper_own[...])
    steps = rows_dev // nb
    count = jnp.int32(0)
    for b in range(steps):
        lanes = pl.ds(b * nb, nb)
        for k, block in zip(order, blocks):
            whole[b % 2, pl.ds(pl.multiple_of((col ^ k) * cw, 8), cw), :] = block[:, lanes]
        for p in range(b * nb // steps, (b + 1) * nb // steps):
            there = pivots[p] - first
            owned_list[count] = there + (p << 16)
            count = count + (there.astype(jnp.uint32) < jnp.uint32(rows_dev)).astype(I32)
        data = whole[b % 2]
        place = lax.broadcasted_iota(I32, (nb, nb), 0) + b * nb
        hit = jnp.max(jnp.where(place == target, 1.0, 0.0), axis=1, keepdims=True)
        fac = jnp.where(hit > 0.5, 0.0, mm3(split2(data.T), tri))
        fac_hi[lanes, :], fac_lo[lanes, :] = split2(fac)
        own_out[:, lanes] = mm3(own, split2(data))
    last = owned_list[jnp.maximum(count - 1, 0)]
    for i in range(GROUP_ROWS):
        owned_list[count + i] = last
    owned_list[wide] = count


def head_kernel(order, pivot_row, *rest):
    heads, (upper, upper_own, own_in, top_hi, top_lo, own_out, top) = (
        rest[: len(order)],
        rest[len(order) :],
    )
    cw, rows_dev = own_in.shape
    nb = upper.shape[0]
    col = lax.axis_index("col")
    for k, head in zip(order, heads):
        top[pl.ds(pl.multiple_of((col ^ k) * cw, 8), cw), :] = head[...]
    data = top[...]
    top_hi[...], top_lo[...] = split2(mm3(split2(data.T), triangle(upper)))
    parts = split3(mm3(split2(upper_own[...]), split2(data)))
    left = jnp.concatenate([*parts, jnp.ones((16, nb), BF16)])
    target = pivot_row[...] - lax.axis_index("row") * rows_dev
    for b in range(rows_dev // nb):
        part = pl.ds(b * nb, nb)
        moved = mm(left, one_hot(target, b * nb, nb), ((1,), (1,)))
        new = (moved[:cw] + moved[cw : 2 * cw]) + moved[2 * cw : 3 * cw]
        own_out[:, part] = jnp.where(moved[3 * cw : 3 * cw + 1] > 0.5, new, own_in[:, part])


def final_kernel(owned_list, look, fac_hi, fac_lo, top_hi, top_lo, lower, pivot_row, *rest):
    picks, spread = rest[:GROUP], rest[GROUP : 2 * GROUP]
    _, updated, panel_out, sketch_out, buf, piv, got, extra, column, in_sem, out_sem, top_sem = rest[2 * GROUP :]
    row = lax.axis_index("row")
    q = lax.rem(row, GROUP)
    slots = pivot_row.shape[1]
    chunk = slots // GROUP
    rows_dev = buf.shape[0]
    extra_rows = extra.shape[0] // GROUP
    blocks = rows_dev // slots

    def load(b):
        part = pl.ds(b * slots, slots)
        return pltpu.make_async_copy(look.at[part, :], buf.at[part, :], in_sem.at[b])

    def store(b):
        part = pl.ds(b * slots, slots)
        return pltpu.make_async_copy(buf.at[part, :], updated.at[part, :], out_sem.at[b])

    for b in range(blocks):
        load(b).start()
    there = pivot_row[...] - row * rows_dev
    here = jnp.where((there >= 0) & (there < rows_dev), 1.0, 0.0)
    column[...] = jnp.broadcast_to(here, (128, slots)).T
    for s in range(GROUP):
        part = pl.ds(pl.multiple_of((q ^ s) * chunk, 8), chunk)
        mine = column[part, :1] > 0.5
        there = spread[s][:chunk, :]
        piv[part, :] = jnp.where(mine, picks[s][:chunk, :], there)
        got[part, :] = there
        erows = pl.ds(pl.multiple_of((q ^ s) * extra_rows, 8), extra_rows)
        extra[erows, :] = spread[s][chunk : chunk + extra_rows, :]
    split = sketch_out.shape[1]
    sketch_out[...] = extra[:, :split]

    below = lax.broadcasted_iota(I32, (slots, slots), 0) > lax.broadcasted_iota(I32, (slots, slots), 1)
    low = split2(jnp.where(below, lower[...], 0.0))
    first = piv[...]
    u_rows = first + mm3(low, split2(first))
    u_hi, u_lo = split2(u_rows)

    load(0).wait()

    @pl.when(owned_list[slots + GROUP_ROWS] > 0)
    def _():
        base = jnp.where(row == 0, buf[:slots, :], got[...])
        got[...] = base - mm3((top_hi[...], top_lo[...]), (u_hi, u_lo))

    for b in range(1, blocks):
        load(b).wait()
    place_rows(owned_list, slots, got, buf)

    for b in range(blocks):
        part = pl.ds(b * slots, slots)
        drop = mm3((fac_hi[part, :], fac_lo[part, :]), (u_hi, u_lo))
        new = buf[part, :] - drop
        if b == 0:
            new = jnp.where(row == 0, u_rows, new)
        buf[part, :] = new
        store(b).start()

    top = pltpu.make_async_copy(
        extra.at[:, pl.ds(split, slots)], panel_out.at[:, pl.ds(0, slots)], top_sem
    )

    @pl.when(row == 0)
    def _():
        top.start()
        top.wait()

    for b in range(blocks):
        store(b).wait()


def on_device(n_row, n_col, panel_col, look_cols, sketch_map, upper_inv, lower_inv, pivots):
    rows_dev, cw = panel_col.shape
    lw = look_cols.shape[1]
    nb, ks = upper_inv.shape[0], sketch_map.shape[0]
    assert rows_dev <= 1 << 16 and nb < 1 << 15
    chunk, extra_rows = nb // GROUP, cw // GROUP
    assert ks + nb == lw and n_row % GROUP == 0
    assert n_row & (n_row - 1) == 0 and n_col & (n_col - 1) == 0
    row, col = lax.axis_index("row"), lax.axis_index("col")
    q = row % GROUP
    panel_t = panel_col.T
    owner = pivots // rows_dev
    pivot_row = pivots.reshape(1, nb)

    def across(v, s):
        return lax.ppermute(v, "row", [(i, i ^ s) for i in range(n_row)])

    message = jax.ShapeDtypeStruct((chunk + extra_rows, lw), F32)
    *picks, head = pl.pallas_call(
        pick_kernel,
        out_shape=[message] * GROUP
        + [jax.ShapeDtypeStruct((cw, nb), F32)],
        in_specs=[SMEM, FAR, FAR, FAR, VMEM],
        out_specs=[VMEM] * (GROUP + 1),
        scratch_shapes=[
            pltpu.VMEM((cw, rows_dev), F32),
            pltpu.VMEM((ks, rows_dev), F32),
            pltpu.VMEM((cw, lw), F32),
            pltpu.SemaphoreType.DMA((GROUP,)),
            pltpu.SemaphoreType.DMA((2 * GROUP,)),
        ],
        cost_estimate=pl.CostEstimate(flops=10**9, bytes_accessed=4 * 10**6, transcendentals=0),
        compiler_params=pltpu.CompilerParams(vmem_limit_bytes=PICK_VMEM),
        name="pick",
    )(pivots, look_cols, panel_t, sketch_map, pivot_row)

    slot_owner = lax.dynamic_slice_in_dim(owner, q * chunk, chunk)
    slot_owner = jnp.concatenate([slot_owner, jnp.full((extra_rows,), -1, I32)])[:, None]
    summed = slot_owner < 0
    got = [picks[0]] + [across(picks[s], s) for s in range(1, GROUP)]
    have = sum(jnp.where(summed | (slot_owner == (row ^ s)), got[s], 0.0) for s in range(GROUP))
    top = got[0]
    for s in range(1, GROUP):
        top = jnp.where(row == s, got[s], top)
    bit = GROUP
    while bit < n_row:
        inside = summed | (slot_owner // bit == row // bit)
        got = across(jnp.where(inside, have, top), bit)
        other = (row // bit) ^ 1
        theirs = slot_owner // bit == other
        have = jnp.where(theirs, 0.0, have) + jnp.where(summed | theirs, got, 0.0)
        top = jnp.where(other == 0, got, top)
        bit *= 2
    spread = [jnp.where(slot_owner == (row ^ s), top, have) for s in range(GROUP)]
    spread = spread[:1] + [across(spread[s], s) for s in range(1, GROUP)]

    blocks = {0: panel_t}
    bit = n_col // 2
    while bit:
        for k in list(blocks):
            pairs = [(i, i ^ bit) for i in range(n_col)]
            blocks[k ^ bit] = lax.ppermute(blocks[k], "col", pairs)
        bit //= 2
    bit = 1
    while bit < n_row:
        sent = lax.ppermute(head, "row", [(i, i + bit) for i in range(bit)])
        head = jnp.where(row // bit == 1, sent, head)
        bit *= 2
    heads = {0: head}
    bit = n_col // 2
    while bit:
        pairs = [(i, i ^ bit) for i in range(n_col)]
        for k in list(heads):
            heads[k ^ bit] = lax.ppermute(heads[k], "col", pairs)
        bit //= 2
    order = list(heads)
    blocks = [blocks[k] for k in order]
    upper_own = lax.dynamic_slice_in_dim(jnp.triu(upper_inv), col * cw, cw, 1).T
    own_shape = jax.ShapeDtypeStruct((cw, rows_dev), F32)
    fac_hi, fac_lo, own_raw, owned_list = pl.pallas_call(
        functools.partial(factor_kernel, order),
        out_shape=[jax.ShapeDtypeStruct((rows_dev, nb), BF16)] * 2
        + [own_shape, jax.ShapeDtypeStruct((nb + 2 * GROUP_ROWS,), I32)],
        in_specs=[SMEM] + [VMEM] * (n_col + 3),
        out_specs=[VMEM] * 3 + [SMEM],
        scratch_shapes=[pltpu.VMEM((2, nb, nb), F32)],
        cost_estimate=pl.CostEstimate(flops=10**9, bytes_accessed=4 * 10**6, transcendentals=0),
        compiler_params=pltpu.CompilerParams(vmem_limit_bytes=FACTOR_VMEM),
        name="factor",
    )(pivots, pivot_row, *blocks, upper_inv, upper_own)
    top_hi, top_lo, panel_out = pl.pallas_call(
        functools.partial(head_kernel, order),
        out_shape=[jax.ShapeDtypeStruct((nb, nb), BF16)] * 2 + [own_shape],
        in_specs=[VMEM] * (4 + n_col),
        out_specs=[VMEM] * 3,
        scratch_shapes=[pltpu.VMEM((nb, nb), F32)],
        cost_estimate=pl.CostEstimate(flops=10**9, bytes_accessed=4 * 10**6, transcendentals=0),
        compiler_params=pltpu.CompilerParams(vmem_limit_bytes=FACTOR_VMEM),
        name="headfix",
    )(pivot_row, *heads.values(), upper_inv, upper_own, own_raw)

    n_in = 8 + 2 * GROUP
    updated, panel_out, sketch_t = pl.pallas_call(
        final_kernel,
        out_shape=[
            jax.ShapeDtypeStruct((rows_dev, lw), F32),
            jax.ShapeDtypeStruct((cw, rows_dev), F32),
            jax.ShapeDtypeStruct((cw, ks), F32),
        ],
        in_specs=[SMEM, HBM] + [VMEM] * (6 + 2 * GROUP) + [HBM],
        out_specs=[HBM, HBM, VMEM],
        input_output_aliases={n_in: 1},
        scratch_shapes=[
            pltpu.VMEM((rows_dev, lw), F32),
            pltpu.VMEM((nb, lw), F32),
            pltpu.VMEM((nb, lw), F32),
            pltpu.VMEM((cw, lw), F32),
            pltpu.VMEM((nb, 128), F32),
            pltpu.SemaphoreType.DMA((rows_dev // nb,)),
            pltpu.SemaphoreType.DMA((rows_dev // nb,)),
            pltpu.SemaphoreType.DMA,
        ],
        cost_estimate=pl.CostEstimate(flops=2 * 10**9, bytes_accessed=12 * 10**6, transcendentals=0),
        compiler_params=pltpu.CompilerParams(vmem_limit_bytes=FINAL_VMEM),
        name="final",
    )(owned_list, look_cols, fac_hi, fac_lo, top_hi, top_lo, lower_inv, pivot_row, *picks, *spread, panel_out)
    return panel_out.T, updated, sketch_t.T


def solution(mesh):
    n_row, n_col = mesh.shape["row"], mesh.shape["col"]
    placed = (P("row", "col"), P("row", "col"), P(None, "row"), P(), P(), P())

    def step(*args):
        return on_device(n_row, n_col, *args)

    return jax.shard_map(
        step,
        mesh=mesh,
        in_specs=placed,
        out_specs=(P("row", "col"), P("row", "col"), P(None, "col")),
        check_vma=False,
    )
```

```python
import functools

import jax
import jax.numpy as jnp
from jax import lax
from jax.experimental import pallas as pl
from jax.experimental.pallas import tpu as pltpu
from jax.sharding import PartitionSpec as P


F32, BF16, I32 = jnp.float32, jnp.bfloat16, jnp.int32
GROUP = 4
GROUP_ROWS = 8
PICK_VMEM = 54_000_000
FACTOR_VMEM = 12_000_000
FINAL_VMEM = 20_000_000
VMEM = pl.BlockSpec(memory_space=pltpu.VMEM)
SMEM = pl.BlockSpec(memory_space=pltpu.SMEM)
HBM = pl.BlockSpec(memory_space=pl.ANY)
FAR = pl.BlockSpec(memory_space=pltpu.HBM)


def split2(x):
    hi = x.astype(BF16)
    return hi, (x - hi.astype(F32)).astype(BF16)


def split3(x):
    hi = x.astype(BF16)
    rest = x - hi.astype(F32)
    mid = rest.astype(BF16)
    return hi, mid, (rest - mid.astype(F32)).astype(BF16)


def mm(a, b, dims=((1,), (0,))):
    return lax.dot_general(a, b, (dims, ((), ())), preferred_element_type=F32)


def mm3(a, b, dims=((1,), (0,))):
    left = jnp.concatenate([a[0], a[0], a[1]], axis=dims[0][0])
    right = jnp.concatenate([b[0], b[1], b[0]], axis=dims[1][0])
    return mm(left, right, dims)


def pick_kernel(pivots, look, panel, sketch_map, pivot_row, *rest):
    outs, (head, pan, ske, extra, sem, in_sem) = rest[:GROUP], rest[GROUP:]
    slots = pivot_row.shape[1]
    rows_dev = panel.shape[1]
    chunk = slots // GROUP
    extra_rows = extra.shape[0] // GROUP
    split = sketch_map.shape[0]
    step = rows_dev // GROUP
    row = lax.axis_index("row")
    q = lax.rem(row, GROUP)
    first = row * rows_dev

    def loads(k):
        part = pl.ds(k * step, step)
        return (
            pltpu.make_async_copy(panel.at[:, part], pan.at[:, part], in_sem.at[k]),
            pltpu.make_async_copy(sketch_map.at[:, part], ske.at[:, part], in_sem.at[GROUP + k]),
        )

    for k in range(GROUP):
        for copy in loads(k):
            copy.start()
    target = pivot_row[...] - first
    sketch_sum = jnp.zeros((panel.shape[0], split), F32)
    pick_sum = jnp.zeros((panel.shape[0], slots), F32)
    for s in range(GROUP):
        base = (q ^ s) * chunk
        for i in range(chunk):
            there = pivots[base + i] - first
            owned = there.astype(jnp.uint32) < jnp.uint32(rows_dev)
            pltpu.make_async_copy(
                look.at[pl.ds(jnp.where(owned, there, base + i), 1), :],
                outs[s].at[pl.ds(i, 1), :],
                sem.at[s],
            ).start()
        for copy in loads(s):
            copy.wait()
        k = s * step
        hi, mid, lo = split3(pan[:, k : k + step])
        sketch_sum += mm3((hi, mid), split2(ske[:, k : k + step]), ((1,), (1,)))
        hot = one_hot(target, k, step)
        pick_sum += (mm(hi, hot) + mm(mid, hot)) + mm(lo, hot)
    head[...] = pan[:, :slots]
    extra[:, :split] = sketch_sum
    extra[:, split:] = pick_sum
    for s in range(GROUP):
        rows = pl.ds(pl.multiple_of((q ^ s) * extra_rows, 8), extra_rows)
        outs[s][chunk : chunk + extra_rows, :] = extra[rows, :]
    for s in range(GROUP):
        pltpu.make_async_copy(
            look.at[pl.ds(0, chunk), :], outs[s].at[pl.ds(0, chunk), :], sem.at[s]
        ).wait()


def one_hot(target, k, step):
    place = lax.broadcasted_iota(I32, (step, target.shape[1]), 0) + k
    return jnp.where(place == target, 1.0, 0.0).astype(BF16)


def place_rows(owned_list, slots, source, out):
    @pl.loop(0, pl.cdiv(owned_list[slots + GROUP_ROWS], GROUP_ROWS))
    def _(k):
        entries = [owned_list[k * GROUP_ROWS + i] for i in range(GROUP_ROWS)]
        rows = [source[pl.ds(entry >> 16, 1), :] for entry in entries]
        for entry, value in zip(entries, rows):
            out[pl.ds(entry & 0xFFFF, 1), :] = value


def triangle(upper):
    shape = upper.shape
    keep = lax.broadcasted_iota(I32, shape, 0) <= lax.broadcasted_iota(I32, shape, 1)
    return split2(jnp.where(keep, upper[...], 0.0))


def factor_kernel(order, pivot_row, *rest):
    blocks, (upper, upper_own, fac_hi, fac_lo, own_out, whole) = (
        rest[: len(order)],
        rest[len(order) :],
    )
    cw, rows_dev = blocks[0].shape
    nb = upper.shape[0]
    col = lax.axis_index("col")
    first = lax.axis_index("row") * rows_dev
    target = pivot_row[...] - first
    tri = triangle(upper)
    own = split2(upper_own[...])
    for b in range(rows_dev // nb):
        lanes = pl.ds(b * nb, nb)
        for k, block in zip(order, blocks):
            whole[b % 2, pl.ds(pl.multiple_of((col ^ k) * cw, 8), cw), :] = block[:, lanes]
        data = whole[b % 2]
        place = lax.broadcasted_iota(I32, (nb, nb), 0) + b * nb
        hit = jnp.max(jnp.where(place == target, 1.0, 0.0), axis=1, keepdims=True)
        fac = jnp.where(hit > 0.5, 0.0, mm3(split2(data.T), tri))
        fac_hi[lanes, :], fac_lo[lanes, :] = split2(fac)
        own_out[:, lanes] = mm3(own, split2(data))


def head_kernel(order, pivots, pivot_row, *rest):
    heads, (upper, upper_own, own_in, top_hi, top_lo, own_out, owned_list, top) = (
        rest[: len(order)],
        rest[len(order) :],
    )
    cw, rows_dev = own_in.shape
    nb = upper.shape[0]
    col = lax.axis_index("col")
    for k, head in zip(order, heads):
        top[pl.ds(pl.multiple_of((col ^ k) * cw, 8), cw), :] = head[...]
    data = top[...]
    top_hi[...], top_lo[...] = split2(mm3(split2(data.T), triangle(upper)))
    parts = split3(mm3(split2(upper_own[...]), split2(data)))
    left = jnp.concatenate([*parts, jnp.ones((16, nb), BF16)])
    first = lax.axis_index("row") * rows_dev
    target = pivot_row[...] - first
    wide = nb + GROUP_ROWS
    steps = rows_dev // nb
    count = jnp.int32(0)
    for b in range(steps):
        for p in range(b * nb // steps, (b + 1) * nb // steps):
            there = pivots[p] - first
            owned_list[count] = there + (p << 16)
            count = count + (there.astype(jnp.uint32) < jnp.uint32(rows_dev)).astype(I32)
        part = pl.ds(b * nb, nb)
        moved = mm(left, one_hot(target, b * nb, nb), ((1,), (1,)))
        new = (moved[:cw] + moved[cw : 2 * cw]) + moved[2 * cw : 3 * cw]
        own_out[:, part] = jnp.where(moved[3 * cw : 3 * cw + 1] > 0.5, new, own_in[:, part])
    last = owned_list[jnp.maximum(count - 1, 0)]
    for i in range(GROUP_ROWS):
        owned_list[count + i] = last
    owned_list[wide] = count


def final_kernel(owned_list, look, fac_hi, fac_lo, top_hi, top_lo, lower, pivot_row, *rest):
    picks, spread = rest[:GROUP], rest[GROUP : 2 * GROUP]
    _, updated, panel_out, sketch_out, buf, piv, got, extra, column, in_sem, out_sem, top_sem = rest[2 * GROUP :]
    row = lax.axis_index("row")
    q = lax.rem(row, GROUP)
    slots = pivot_row.shape[1]
    chunk = slots // GROUP
    rows_dev = buf.shape[0]
    extra_rows = extra.shape[0] // GROUP
    blocks = rows_dev // slots

    def load(b):
        part = pl.ds(b * slots, slots)
        return pltpu.make_async_copy(look.at[part, :], buf.at[part, :], in_sem.at[b])

    def store(b):
        part = pl.ds(b * slots, slots)
        return pltpu.make_async_copy(buf.at[part, :], updated.at[part, :], out_sem.at[b])

    for b in range(blocks):
        load(b).start()
    there = pivot_row[...] - row * rows_dev
    here = jnp.where((there >= 0) & (there < rows_dev), 1.0, 0.0)
    column[...] = jnp.broadcast_to(here, (128, slots)).T
    for s in range(GROUP):
        part = pl.ds(pl.multiple_of((q ^ s) * chunk, 8), chunk)
        mine = column[part, :1] > 0.5
        there = spread[s][:chunk, :]
        piv[part, :] = jnp.where(mine, picks[s][:chunk, :], there)
        got[part, :] = there
        erows = pl.ds(pl.multiple_of((q ^ s) * extra_rows, 8), extra_rows)
        extra[erows, :] = spread[s][chunk : chunk + extra_rows, :]
    split = sketch_out.shape[1]
    sketch_out[...] = extra[:, :split]

    below = lax.broadcasted_iota(I32, (slots, slots), 0) > lax.broadcasted_iota(I32, (slots, slots), 1)
    low = split2(jnp.where(below, lower[...], 0.0))
    first = piv[...]
    u_rows = first + mm3(low, split2(first))
    u_hi, u_lo = split2(u_rows)

    load(0).wait()

    @pl.when(owned_list[slots + GROUP_ROWS] > 0)
    def _():
        base = jnp.where(row == 0, buf[:slots, :], got[...])
        got[...] = base - mm3((top_hi[...], top_lo[...]), (u_hi, u_lo))

    for b in range(1, blocks):
        load(b).wait()
    place_rows(owned_list, slots, got, buf)

    for b in range(blocks):
        part = pl.ds(b * slots, slots)
        drop = mm3((fac_hi[part, :], fac_lo[part, :]), (u_hi, u_lo))
        new = buf[part, :] - drop
        if b == 0:
            new = jnp.where(row == 0, u_rows, new)
        buf[part, :] = new
        store(b).start()

    top = pltpu.make_async_copy(
        extra.at[:, pl.ds(split, slots)], panel_out.at[:, pl.ds(0, slots)], top_sem
    )

    @pl.when(row == 0)
    def _():
        top.start()
        top.wait()

    for b in range(blocks):
        store(b).wait()


def on_device(n_row, n_col, panel_col, look_cols, sketch_map, upper_inv, lower_inv, pivots):
    rows_dev, cw = panel_col.shape
    lw = look_cols.shape[1]
    nb, ks = upper_inv.shape[0], sketch_map.shape[0]
    assert rows_dev <= 1 << 16 and nb < 1 << 15
    chunk, extra_rows = nb // GROUP, cw // GROUP
    assert ks + nb == lw and n_row % GROUP == 0
    assert n_row & (n_row - 1) == 0 and n_col & (n_col - 1) == 0
    row, col = lax.axis_index("row"), lax.axis_index("col")
    q = row % GROUP
    panel_t = panel_col.T
    owner = pivots // rows_dev
    pivot_row = pivots.reshape(1, nb)

    def across(v, s):
        return lax.ppermute(v, "row", [(i, i ^ s) for i in range(n_row)])

    message = jax.ShapeDtypeStruct((chunk + extra_rows, lw), F32)
    *picks, head = pl.pallas_call(
        pick_kernel,
        out_shape=[message] * GROUP
        + [jax.ShapeDtypeStruct((cw, nb), F32)],
        in_specs=[SMEM, FAR, FAR, FAR, VMEM],
        out_specs=[VMEM] * (GROUP + 1),
        scratch_shapes=[
            pltpu.VMEM((cw, rows_dev), F32),
            pltpu.VMEM((ks, rows_dev), F32),
            pltpu.VMEM((cw, lw), F32),
            pltpu.SemaphoreType.DMA((GROUP,)),
            pltpu.SemaphoreType.DMA((2 * GROUP,)),
        ],
        cost_estimate=pl.CostEstimate(flops=10**9, bytes_accessed=4 * 10**6, transcendentals=0),
        compiler_params=pltpu.CompilerParams(vmem_limit_bytes=PICK_VMEM),
        name="pick",
    )(pivots, look_cols, panel_t, sketch_map, pivot_row)

    slot_owner = lax.dynamic_slice_in_dim(owner, q * chunk, chunk)
    slot_owner = jnp.concatenate([slot_owner, jnp.full((extra_rows,), -1, I32)])[:, None]
    summed = slot_owner < 0
    got = [picks[0]] + [across(picks[s], s) for s in range(1, GROUP)]
    have = sum(jnp.where(summed | (slot_owner == (row ^ s)), got[s], 0.0) for s in range(GROUP))
    top = got[0]
    for s in range(1, GROUP):
        top = jnp.where(row == s, got[s], top)
    bit = GROUP
    while bit < n_row:
        inside = summed | (slot_owner // bit == row // bit)
        got = across(jnp.where(inside, have, top), bit)
        other = (row // bit) ^ 1
        theirs = slot_owner // bit == other
        have = jnp.where(theirs, 0.0, have) + jnp.where(summed | theirs, got, 0.0)
        top = jnp.where(other == 0, got, top)
        bit *= 2
    spread = [jnp.where(slot_owner == (row ^ s), top, have) for s in range(GROUP)]
    spread = spread[:1] + [across(spread[s], s) for s in range(1, GROUP)]

    blocks = {0: panel_t}
    bit = n_col // 2
    while bit:
        for k in list(blocks):
            pairs = [(i, i ^ bit) for i in range(n_col)]
            blocks[k ^ bit] = lax.ppermute(blocks[k], "col", pairs)
        bit //= 2
    bit = 1
    while bit < n_row:
        sent = lax.ppermute(head, "row", [(i, i + bit) for i in range(bit)])
        head = jnp.where(row // bit == 1, sent, head)
        bit *= 2
    heads = {0: head}
    bit = n_col // 2
    while bit:
        pairs = [(i, i ^ bit) for i in range(n_col)]
        for k in list(heads):
            heads[k ^ bit] = lax.ppermute(heads[k], "col", pairs)
        bit //= 2
    order = list(heads)
    blocks = [blocks[k] for k in order]
    upper_own = lax.dynamic_slice_in_dim(jnp.triu(upper_inv), col * cw, cw, 1).T
    own_shape = jax.ShapeDtypeStruct((cw, rows_dev), F32)
    fac_hi, fac_lo, own_raw = pl.pallas_call(
        functools.partial(factor_kernel, order),
        out_shape=[jax.ShapeDtypeStruct((rows_dev, nb), BF16)] * 2
        + [own_shape],
        in_specs=[VMEM] * (n_col + 3),
        out_specs=[VMEM] * 3,
        scratch_shapes=[pltpu.VMEM((2, nb, nb), F32)],
        cost_estimate=pl.CostEstimate(flops=10**9, bytes_accessed=4 * 10**6, transcendentals=0),
        compiler_params=pltpu.CompilerParams(vmem_limit_bytes=FACTOR_VMEM),
        name="factor",
    )(pivot_row, *blocks, upper_inv, upper_own)
    top_hi, top_lo, panel_out, owned_list = pl.pallas_call(
        functools.partial(head_kernel, order),
        out_shape=[jax.ShapeDtypeStruct((nb, nb), BF16)] * 2
        + [own_shape, jax.ShapeDtypeStruct((nb + 2 * GROUP_ROWS,), I32)],
        in_specs=[SMEM] + [VMEM] * (4 + n_col),
        out_specs=[VMEM] * 3 + [SMEM],
        scratch_shapes=[pltpu.VMEM((nb, nb), F32)],
        cost_estimate=pl.CostEstimate(flops=10**9, bytes_accessed=4 * 10**6, transcendentals=0),
        compiler_params=pltpu.CompilerParams(vmem_limit_bytes=FACTOR_VMEM),
        name="headfix",
    )(pivots, pivot_row, *heads.values(), upper_inv, upper_own, own_raw)

    n_in = 8 + 2 * GROUP
    updated, panel_out, sketch_t = pl.pallas_call(
        final_kernel,
        out_shape=[
            jax.ShapeDtypeStruct((rows_dev, lw), F32),
            jax.ShapeDtypeStruct((cw, rows_dev), F32),
            jax.ShapeDtypeStruct((cw, ks), F32),
        ],
        in_specs=[SMEM, HBM] + [VMEM] * (6 + 2 * GROUP) + [HBM],
        out_specs=[HBM, HBM, VMEM],
        input_output_aliases={n_in: 1},
        scratch_shapes=[
            pltpu.VMEM((rows_dev, lw), F32),
            pltpu.VMEM((nb, lw), F32),
            pltpu.VMEM((nb, lw), F32),
            pltpu.VMEM((cw, lw), F32),
            pltpu.VMEM((nb, 128), F32),
            pltpu.SemaphoreType.DMA((rows_dev // nb,)),
            pltpu.SemaphoreType.DMA((rows_dev // nb,)),
            pltpu.SemaphoreType.DMA,
        ],
        cost_estimate=pl.CostEstimate(flops=2 * 10**9, bytes_accessed=12 * 10**6, transcendentals=0),
        compiler_params=pltpu.CompilerParams(vmem_limit_bytes=FINAL_VMEM),
        name="final",
    )(owned_list, look_cols, fac_hi, fac_lo, top_hi, top_lo, lower_inv, pivot_row, *picks, *spread, panel_out)
    return panel_out.T, updated, sketch_t.T


def solution(mesh):
    n_row, n_col = mesh.shape["row"], mesh.shape["col"]
    placed = (P("row", "col"), P("row", "col"), P(None, "row"), P(), P(), P())

    def step(*args):
        return on_device(n_row, n_col, *args)

    return jax.shard_map(
        step,
        mesh=mesh,
        in_specs=placed,
        out_specs=(P("row", "col"), P("row", "col"), P(None, "col")),
        check_vma=False,
    )
```
